32 devices in a mesh: member: 2 (over x), lateral: 8 (over z, y), radial: 2 (over core).
Axes of the slice: x: 2, y: 2, z: 4, core: 2. Of those that a mesh axis runs over, the one named last changes fastest.
Arguments:
- initial_displacement: float32 [6, 8, 256, 2048], P('member', 'radial', 'lateral'), parts along dimension 0, may hold values from -6 to 6
- force: float32 [6, 8, 256, 2048], P('member', 'radial', 'lateral'), parts along dimension 0, may hold values from -12 to 12
- viscosity: float32 [32], P('member'), parts along dimension 0, may hold values from 0.1 to 10
- layer_index: int32 [8, 256, 2048], P('radial', 'lateral'), may hold values from 0 to 15
- response: float32 [512, 1024], P(None, 'lateral'), may hold values from 0.2 to 2
- ocean_mask: int32 [256, 2048], P('lateral'), may hold values 0 or 1
Outputs:
- displacement: float32 [6, 8, 256, 2048], P('member', 'radial', 'lateral'), parts along dimension 0
- coefficients: float32 [1024, 1024], P('member', ('lateral', 'radial')), parts along dimension 0
- sea_load: float32 [256, 4096], P('lateral', 'member'), parts along dimension 1
The draws below stay inside these ranges and needn't reach their ends.
There are 2 independent parts, one for each index of `member`. The reference program is written for one: setup_inputs(seed, part) draws one part's arguments, and reference() takes and returns one part's arrays. A program takes and returns all parts, laid end to end along the dimension named above; an argument that names none is the same for every part. Nothing has to cross between parts.
All inputs are finite; a program needn't handle non-finite values. No bound on the sum of `ocean_mask` on one device may be relied on, other than what follows from the above.
Results may differ from the reference program's by a relative error of at most 0.000073.
Values sent between devices are 32-bit elements; how exact they have to be, the bound alone decides.
A program may use at most 128 MiB of HBM per device.

```python
import math
import jax
import jax.numpy as jnp
from jax import lax

SHELLS = 8
NLON = 2048
MODES = 512
LAYERS = 16
SWEEPS = 2
NLAT = 256


def with_ends(values, own_key, low, top_value):
    dims = values.shape
    spot = [jax.random.randint(jax.random.fold_in(own_key, axis), (), 0, dims[axis]) for axis in range(len(dims))]
    values = values.at[tuple(spot)].set(low)
    longest = dims.index(max(dims))
    spot[longest] = (spot[longest] + 1) % dims[longest]
    return values.at[tuple(spot)].set(top_value)


def levels(stream_key, shape, cuts, least, largest):
    factor_of, own = 1.0, jax.random.fold_in(stream_key, 6)
    for position, shards_of in cuts:
        draws = jnp.exp(jax.random.uniform(jax.random.fold_in(own, position), (shards_of,), jnp.float32, least / len(cuts), largest / len(cuts)))
        factor_of = factor_of * jnp.repeat(draws, shape[position] // shards_of).reshape([-1 if axis == position else 1 for axis in range(len(shape))])
    return factor_of


def noise(key, dims, deviation, limit, split=(), kind=jnp.bfloat16):
    loudness = levels(key, dims, split, -0.22, 0.18) if split else 1.0
    values = jax.random.normal(key, dims, jnp.float32) * deviation * loudness
    return jnp.minimum(jnp.maximum(values, -limit), limit).astype(kind)


def setup_inputs(seed: int = 0, part: int = 0) -> dict:
    seeds = jax.random.split(jax.random.key(seed), 7)
    own_keys = jax.random.split(jax.random.fold_in(seeds[6], part), 7)
    initial_displacement = noise(own_keys[0], (3, SHELLS, NLAT, NLON), 1.0, 6.0, ((1, 2), (2, 8)), jnp.float32)
    force = noise(own_keys[1], (3, SHELLS, NLAT, NLON), 2.0, 12.0, ((1, 2), (2, 8)), jnp.float32)
    viscosity = jnp.clip(jnp.exp(jax.random.uniform(own_keys[2], (LAYERS,), jnp.float32, math.log(0.1), math.log(10.0))), 0.1, 10.0)
    layer_index = with_ends(jax.random.randint(seeds[3], (SHELLS, NLAT, NLON), 0, LAYERS), jax.random.fold_in(seeds[3], 1), 0, LAYERS - 1).astype(jnp.int32)
    response = jnp.clip(jnp.exp(math.log(2.0) - 2.3025851 * jax.random.uniform(seeds[4], (MODES, 2 * MODES), jnp.float32) ** levels(seeds[4], (MODES, 2 * MODES), ((1, 8),), -0.2, 0.2)), 0.2, 2.0)
    ocean_mask = with_ends((jax.random.randint(seeds[5], (NLAT, NLON), 0, 10) < 7).astype(jnp.int32), jax.random.fold_in(seeds[5], 1), 0, 1)
    return dict(initial_displacement=initial_displacement, force=force, viscosity=viscosity, layer_index=layer_index, response=response, ocean_mask=ocean_mask)


highest = lax.Precision.HIGHEST
relaxation = 0.8

def layer_lookup(layer_index, viscosity):
    result = jnp.zeros(layer_index.shape, jnp.float32)
    for layer_number in range(viscosity.shape[0]):
        result = result + jnp.where(layer_index == layer_number, viscosity[layer_number], jnp.zeros((), viscosity.dtype))
    return result

def longitude_table(count, columns, modes):
    points = jnp.arange(count, dtype=jnp.int32)[:, None]
    orders = (columns % modes)[None, :]
    phase = points * orders % count
    angle = 2.0 * math.pi / count * phase.astype(jnp.float32)
    table = jnp.where(columns[None, :] >= modes, jnp.sin(angle), jnp.cos(angle))
    return table * math.sqrt(2.0 / count)

def colatitude_table(count, modes):
    points = jnp.arange(count, dtype=jnp.int32)[:, None]
    waves = jnp.arange(modes, dtype=jnp.int32)[None, :]
    phase = waves * (2 * points + 1) % (4 * count)
    angle = math.pi / (2 * count) * phase.astype(jnp.float32)
    return jnp.cos(angle) * math.sqrt(2.0 / count)

def sweep(padded, eta_padded, force):
    eta_mid = eta_padded[1:-1, 1:-1]
    middle = padded[:, 1:-1, 1:-1]
    beside_eta = [eta_padded[2:, 1:-1], eta_padded[:-2, 1:-1], eta_padded[1:-1, 2:], eta_padded[1:-1, :-2], jnp.roll(eta_mid, 1, axis=-1), jnp.roll(eta_mid, -1, axis=-1)]
    beside_field = [padded[:, 2:, 1:-1], padded[:, :-2, 1:-1], padded[:, 1:-1, 2:], padded[:, 1:-1, :-2], jnp.roll(middle, 1, axis=-1), jnp.roll(middle, -1, axis=-1)]
    diagonal = jnp.ones(eta_mid.shape, eta_mid.dtype)
    pulled = jnp.zeros(middle.shape, middle.dtype)
    for other_eta, other_field in zip(beside_eta, beside_field):
        weight = 0.5 * (eta_mid + other_eta)
        diagonal = diagonal + weight
        pulled = pulled + weight[None] * other_field
    remainder = force - (diagonal[None] * middle - pulled)
    return middle + relaxation * remainder / diagonal[None]

def reference(initial_displacement, force, viscosity, layer_index, response, ocean_mask):
    eta = layer_lookup(layer_index, viscosity)
    eta_padded = jnp.pad(eta, ((1, 1), (1, 1), (0, 0)))
    displacement = initial_displacement
    for sweep_number in range(SWEEPS):
        padded = jnp.pad(displacement, ((0, 0), (1, 1), (1, 1), (0, 0)))
        displacement = sweep(padded, eta_padded, force)
    surface = displacement[0, SHELLS - 1]
    columns = jnp.arange(2 * MODES, dtype=jnp.int32)
    longitude = longitude_table(NLON, columns, MODES)
    colatitude = colatitude_table(NLAT, MODES)
    fourier = jnp.dot(surface, longitude, precision=highest)
    coefficients = jnp.dot(colatitude.T, fourier, precision=highest)
    load_spectrum = response * coefficients
    load_rows = jnp.dot(colatitude, load_spectrum, precision=highest)
    sea_load = ocean_mask.astype(jnp.float32) * jnp.dot(load_rows, longitude.T, precision=highest)
    return (displacement, coefficients, sea_load)
```

```python
import functools
import math

import jax
import jax.numpy as jnp
import ml_dtypes
import numpy as np
from jax import lax
from jax.experimental import pallas as pl
from jax.experimental.pallas import tpu as pltpu
from jax.sharding import PartitionSpec as P

MODES = 512
PAD = 8
MESH = pl.DeviceIdType.MESH
f32, bf16 = jnp.float32, jnp.bfloat16


def halves(table):
    table = table.astype(np.float32)
    high = table.astype(ml_dtypes.bfloat16)
    low = (table - high.astype(np.float32)).astype(ml_dtypes.bfloat16)
    return high, low


def longitude_quarter(count, modes):
    points = np.arange(count // 4)[:, None]
    phase = points * np.arange(modes)[None, :] % count
    angle = 2.0 * math.pi / count * phase
    table = np.concatenate([np.cos(angle), np.sin(angle)], axis=1)
    return halves(table * math.sqrt(2.0 / count))


def colatitude_table(count, modes):
    points = np.arange(count)[:, None]
    phase = np.arange(modes)[None, :] * (2 * points + 1) % (4 * count)
    table = np.cos(math.pi / (2 * count) * phase) * math.sqrt(2.0 / count)
    return halves(table)


def split(x):
    high = x.astype(bf16)
    return high, (x - high.astype(f32)).astype(bf16)


def dot(a, b, dims=(((1,), (0,)), ((), ()))):
    return lax.dot_general(a, b, dims, preferred_element_type=f32)


def choose(index, values):
    bit = 0
    while len(values) > 1:
        odd = (index & (1 << bit)) != 0
        values = [
            jnp.where(odd, values[min(i + 1, len(values) - 1)], values[i])
            for i in range(0, len(values), 2)
        ]
        bit += 1
    return values[0]


def kernel(lat, rad, layers, disp, force, visc, layer, response, mask, th, tl, ch, cl, cth, ctl,
           out, coef_out, sea_out,
           u0, u1, fv, li, he, r_out, r_in, e_out, e_in, l_out, l_in, surf, fsend, frecv, gsend, grecv, gather,
           resp_v, mask_v, th_v, tl_v, ch_v, cl_v, cth_v, ctl_v,
           load_sem, send_sem, recv_sem, a_send, a_recv, out_sem):
    comps, shells, rows, lon = disp.shape
    width = response.shape[1]
    me = lax.axis_index("lateral")
    place = lax.axis_index("radial")
    inner = pl.ds(PAD, rows)

    def load(source, target, index):
        copy = pltpu.make_async_copy(source, target, load_sem.at[index])
        copy.start()
        return copy

    c_layer = load(layer, li.at[pl.ds(1, shells)], 0)
    c_disp = load(disp, u0.at[:, pl.ds(1, shells), inner], 1)
    c_force = load(force, fv, 2)
    pairs = [(response, resp_v), (mask, mask_v), (th, th_v), (tl, tl_v), (ch, ch_v), (cl, cl_v),
             (cth, cth_v), (ctl, ctl_v)]
    c_tables = [load(a, b, 3 + i) for i, (a, b) in enumerate(pairs)]

    barrier = pltpu.get_barrier_semaphore()
    for d in range(1, lat):
        pl.semaphore_signal(barrier, inc=1, device_id={"lateral": lax.rem(me + d, lat)}, device_id_type=MESH)
    for d in range(1, rad):
        pl.semaphore_signal(barrier, inc=1, device_id={"radial": lax.rem(place + d, rad)}, device_id_type=MESH)
    pl.semaphore_wait(barrier, lat + rad - 2)

    def remote(source, target, sem, axis, where):
        return pltpu.make_async_remote_copy(
            src_ref=source, dst_ref=target, send_sem=send_sem.at[sem], recv_sem=recv_sem.at[sem],
            device_id={axis: where}, device_id_type=MESH)

    above, below = place < rad - 1, place > 0
    south, north = me < lat - 1, me > 0
    up_id, down_id = lax.rem(place + 1, rad), lax.rem(place + rad - 1, rad)
    south_id, north_id = lax.rem(me + 1, lat), lax.rem(me + lat - 1, lat)

    li_up = remote(layer.at[shells - 1], li.at[0], 0, "radial", up_id)
    li_down = remote(layer.at[0], li.at[shells + 1], 1, "radial", down_id)
    d_up = remote(disp.at[:, shells - 1], u0.at[:, 0, inner], 2, "radial", up_id)
    d_down = remote(disp.at[:, 0], u0.at[:, shells + 1, inner], 3, "radial", down_id)

    @pl.when(above)
    def _():
        li_up.start()
        d_up.start()

    @pl.when(below)
    def _():
        li_down.start()
        d_down.start()

    values = [visc[i] * 0.5 for i in range(layers)]

    def lookup(s):
        for r in range(0, rows, 8):
            he[s, PAD + r:PAD + r + 8, :] = choose(li[s, r:r + 8, :], values)

    def lookup_step(i, carry):
        lookup(i + 1)
        return carry

    def stage(field, side, row):
        for c in range(comps):
            for s in range(shells):
                r_out[side, c * shells + s, :] = field[c, s + 1, PAD + row, :]

    def unstage(field, side, row):
        for c in range(comps):
            for s in range(shells):
                field[c, s + 1, row, :] = r_in[side, c * shells + s, :]

    def unstage_zero(field, row):
        for c in range(comps):
            for s in range(shells):
                field[c, s + 1, row, :] = jnp.zeros((lon,), f32)

    c_disp.wait()
    stage(u0, 0, rows - 1)
    stage(u0, 1, 0)
    r_south = remote(r_out.at[0], r_in.at[0], 4, "lateral", south_id)
    r_north = remote(r_out.at[1], r_in.at[1], 5, "lateral", north_id)

    @pl.when(south)
    def _():
        r_south.start()

    @pl.when(north)
    def _():
        r_north.start()

    c_layer.wait()
    lax.fori_loop(0, shells, lookup_step, 0)
    for s in range(shells):
        e_out[0, s, :] = he[s + 1, PAD + rows - 1, :]
        e_out[1, s, :] = he[s + 1, PAD, :]
    e_south = remote(e_out.at[0], e_in.at[0], 6, "lateral", south_id)
    e_north = remote(e_out.at[1], e_in.at[1], 7, "lateral", north_id)

    @pl.when(south)
    def _():
        e_south.start()

    @pl.when(north)
    def _():
        e_north.start()

    @pl.when(below)
    def _():
        li_up.wait_recv()
        lookup(0)
        d_up.wait_recv()

    @pl.when(jnp.logical_not(below))
    def _():
        he[0, PAD:PAD + rows, :] = jnp.zeros((rows, lon), f32)
        for c in range(comps):
            u0[c, 0, PAD:PAD + rows, :] = jnp.zeros((rows, lon), f32)
            u1[c, 0, PAD:PAD + rows, :] = jnp.zeros((rows, lon), f32)

    @pl.when(above)
    def _():
        li_down.wait_recv()
        lookup(shells + 1)
        d_down.wait_recv()

    @pl.when(jnp.logical_not(above))
    def _():
        he[shells + 1, PAD:PAD + rows, :] = jnp.zeros((rows, lon), f32)
        for c in range(comps):
            u0[c, shells + 1, PAD:PAD + rows, :] = jnp.zeros((rows, lon), f32)
            u1[c, shells + 1, PAD:PAD + rows, :] = jnp.zeros((rows, lon), f32)

    @pl.when(north)
    def _():
        r_south.wait_recv()
        e_south.wait_recv()
        unstage(u0, 0, PAD - 1)
        for s in range(shells):
            he[s + 1, PAD - 1, :] = e_in[0, s, :]

    @pl.when(jnp.logical_not(north))
    def _():
        unstage_zero(u0, PAD - 1)
        unstage_zero(u1, PAD - 1)
        for s in range(shells):
            he[s + 1, PAD - 1, :] = jnp.zeros((lon,), f32)

    @pl.when(south)
    def _():
        r_north.wait_recv()
        e_north.wait_recv()
        unstage(u0, 1, PAD + rows)
        for s in range(shells):
            he[s + 1, PAD + rows, :] = e_in[1, s, :]

    @pl.when(jnp.logical_not(south))
    def _():
        unstage_zero(u0, PAD + rows)
        unstage_zero(u1, PAD + rows)
        for s in range(shells):
            he[s + 1, PAD + rows, :] = jnp.zeros((lon,), f32)

    def sweep_shell(src, dst, s):
        for r in range(PAD, PAD + rows, 8):
            h = he[s + 1, r:r + 8, :]
            ws = [
                h + he[s + 2, r:r + 8, :],
                h + he[s, r:r + 8, :],
                h + he[s + 1, r + 1:r + 9, :],
                h + he[s + 1, r - 1:r + 7, :],
                h + pltpu.roll(h, 1, 1),
                h + pltpu.roll(h, lon - 1, 1),
            ]
            rate = 0.8 / (1.0 + (((ws[0] + ws[1]) + (ws[2] + ws[3])) + (ws[4] + ws[5])))
            for c in range(comps):
                u = src[c, s + 1, r:r + 8, :]
                total = fv[c, s, r - PAD:r - PAD + 8, :]
                total = total + ws[0] * src[c, s + 2, r:r + 8, :]
                total = total + ws[1] * src[c, s, r:r + 8, :]
                total = total + ws[2] * src[c, s + 1, r + 1:r + 9, :]
                total = total + ws[3] * src[c, s + 1, r - 1:r + 7, :]
                total = total + ws[4] * pltpu.roll(u, 1, 1)
                total = total + ws[5] * pltpu.roll(u, lon - 1, 1)
                dst[c, s + 1, r:r + 8, :] = 0.2 * u + rate * total

    c_force.wait()

    def first(i, carry):
        sweep_shell(u0, u1, i)
        return carry

    lax.fori_loop(0, shells, first, 0)

    @pl.when(above)
    def _():
        li_up.wait_send()
        d_up.wait_send()

    @pl.when(below)
    def _():
        li_down.wait_send()
        d_down.wait_send()

    @pl.when(south)
    def _():
        r_south.wait_send()
        e_south.wait_send()

    @pl.when(north)
    def _():
        r_north.wait_send()
        e_north.wait_send()

    g_up = remote(u1.at[:, shells, inner], u1.at[:, 0, inner], 8, "radial", up_id)
    g_down = remote(u1.at[:, 1, inner], u1.at[:, shells + 1, inner], 9, "radial", down_id)

    def stage_later(side, row):
        for c in range(comps):
            for s in range(shells):
                l_out[side, c * shells + s, :] = u1[c, s + 1, PAD + row, :]

    def unstage_later(side, row):
        for c in range(comps):
            for s in range(shells):
                u1[c, s + 1, row, :] = l_in[side, c * shells + s, :]

    s_south = remote(l_out.at[0], l_in.at[0], 10, "lateral", south_id)
    s_north = remote(l_out.at[1], l_in.at[1], 11, "lateral", north_id)
    stage_later(0, rows - 1)
    stage_later(1, 0)

    @pl.when(south)
    def _():
        s_south.start()

    @pl.when(north)
    def _():
        s_north.start()

    @pl.when(above)
    def _():
        g_up.start()

    @pl.when(below)
    def _():
        g_down.start()

    @pl.when(north)
    def _():
        s_south.wait_recv()
        unstage_later(0, PAD - 1)

    @pl.when(south)
    def _():
        s_north.wait_recv()
        unstage_later(1, PAD + rows)

    @pl.when(below)
    def _():
        g_up.wait_recv()

    @pl.when(above)
    def _():
        g_down.wait_recv()

    def finish(s):
        return pltpu.make_async_copy(u0.at[:, s + 1, inner], out.at[:, s], out_sem.at[s])

    last = shells - 1
    sweep_shell(u1, u0, last)
    finish(last).start()

    top = place == rad - 1
    others = [
        remote(surf, surf, 12 + d - 1, "radial", lax.rem(place + d, rad)) for d in range(1, rad)
    ]

    @pl.when(top)
    def _():
        surf[...] = u0[0, shells, PAD:PAD + rows, :]
        for copy in others:
            copy.start()

    def second(i, carry):
        sweep_shell(u1, u0, i)
        finish(i).start()
        return carry

    lax.fori_loop(0, 1, second, 0)

    for d in range(1, rad):
        @pl.when(place == d - 1)
        def _(d=d):
            others[rad - d - 1].wait_recv()

    for copy in c_tables:
        copy.wait()

    quarter = lon // 4
    modes = th.shape[1] // 2
    x = jnp.concatenate([surf[:, quarter * m:quarter * (m + 1)] for m in range(4)], axis=0)
    xh, xl = split(x)
    g = dot(xh, th_v[...]) + dot(xl, th_v[...]) + dot(xh, tl_v[...])
    gc = [g[rows * m:rows * (m + 1), :modes] for m in range(4)]
    gs = [g[rows * m:rows * (m + 1), modes:] for m in range(4)]
    wave = lax.broadcasted_iota(jnp.int32, (rows, modes), 1) & 3
    zero, one = jnp.zeros((rows, modes), f32), jnp.ones((rows, modes), f32)
    e1 = jnp.where(wave == 0, one, jnp.where(wave == 2, -one, zero))
    s1 = jnp.where(wave == 1, one, jnp.where(wave == 3, -one, zero))
    e2 = jnp.where((wave & 1) == 0, one, -one)
    fc = gc[0] + e2 * gc[2] + e1 * (gc[1] + gc[3]) - s1 * (gs[1] - gs[3])
    fs = gs[0] + e2 * gs[2] + e1 * (gs[1] + gs[3]) + s1 * (gc[1] - gc[3])
    fourier = jnp.concatenate([fc, fs], axis=1)
    for p in range(lat):
        fsend[p] = fourier[:, p * width:(p + 1) * width]

    def exchange(source, target, base):
        copies = []
        for d in range(1, lat):
            peer = lax.rem(me + d, lat)
            copies.append(pltpu.make_async_remote_copy(
                src_ref=source.at[peer], dst_ref=target.at[me],
                send_sem=a_send.at[base + d], recv_sem=a_recv.at[base + d],
                device_id={"lateral": peer}, device_id_type=MESH))
        for copy in copies:
            copy.start()
        return copies

    copies_f = exchange(fsend, frecv, 0)
    frecv[me] = fsend[me]
    lax.fori_loop(1, shells - 1, second, 0)
    for copy in copies_f:
        copy.wait()

    field = frecv[...].reshape(lat * rows, width)
    fh, fl = split(field)
    coef = dot(cth_v[...], fh) + dot(cth_v[...], fl) + dot(ctl_v[...], fh)
    half = width // rad
    for r in range(rad):
        @pl.when(place == r)
        def _(r=r):
            coef_out[...] = coef[:, r * half:(r + 1) * half]
    sh, sl = split(resp_v[...] * coef)
    load_rows = dot(ch_v[...], sh) + dot(ch_v[...], sl) + dot(cl_v[...], sh)
    gsend[...] = load_rows.reshape(lat, rows, width)
    copies_g = exchange(gsend, grecv, lat)
    grecv[me] = gsend[me]
    for copy in copies_g:
        copy.wait()
    for p in range(lat):
        gather[:, p * width:(p + 1) * width] = grecv[p]
    rc, rs = gather[:, :modes], gather[:, modes:]
    twisted = [
        (rc, rs),
        (e1 * rc + s1 * rs, e1 * rs - s1 * rc),
        (e2 * rc, e2 * rs),
        (e1 * rc - s1 * rs, e1 * rs + s1 * rc),
    ]
    a = jnp.concatenate([jnp.concatenate(pair, axis=1) for pair in twisted], axis=0)
    ah, al = split(a)
    nt = (((1,), (1,)), ((), ()))
    sea = dot(ah, th_v[...], nt) + dot(al, th_v[...], nt) + dot(ah, tl_v[...], nt)
    for m in range(4):
        cut = slice(quarter * m, quarter * (m + 1))
        sea_out[:, cut] = mask_v[:, cut].astype(f32) * sea[rows * m:rows * (m + 1)]

    for s in range(shells):
        finish(s).wait()

    @pl.when(south)
    def _():
        s_south.wait_send()

    @pl.when(north)
    def _():
        s_north.wait_send()

    @pl.when(above)
    def _():
        g_up.wait_send()

    @pl.when(below)
    def _():
        g_down.wait_send()

    @pl.when(top)
    def _():
        for copy in others:
            copy.wait_send()


def shards(lat, rad, disp, force, visc, layer, response, mask):
    comps, shells, rows, lon = disp.shape
    width = response.shape[1]
    th, tl = longitude_quarter(lon, MODES)
    ch, cl = colatitude_table(lat * rows, MODES)
    tables = [th, tl, ch, cl, ch.T.copy(), cl.T.copy()]
    hbm = pl.BlockSpec(memory_space=pltpu.HBM)
    vmem = pl.BlockSpec(memory_space=pltpu.VMEM)
    field = pltpu.VMEM((comps, shells + 2, rows + 2 * PAD, lon), f32)
    staged = [pltpu.VMEM((2, n, lon), f32) for n in (comps * shells, shells, comps * shells) for _ in range(2)]
    block = pltpu.VMEM((lat, rows, width), f32)
    dma = pltpu.SemaphoreType.DMA
    return pl.pallas_call(
        functools.partial(kernel, lat, rad, visc.shape[0]),
        out_shape=(
            jax.ShapeDtypeStruct(disp.shape, f32),
            jax.ShapeDtypeStruct((MODES, width // rad), f32),
            jax.ShapeDtypeStruct((rows, lon), f32),
        ),
        in_specs=[hbm, hbm, pl.BlockSpec(memory_space=pltpu.SMEM)] + [hbm] * 9,
        out_specs=(hbm, vmem, vmem),
        scratch_shapes=[
            field, field,
            pltpu.VMEM((comps, shells, rows, lon), f32),
            pltpu.VMEM((shells + 2, rows, lon), jnp.int32),
            pltpu.VMEM((shells + 2, rows + 2 * PAD, lon), f32),
            *staged,
            pltpu.VMEM((rows, lon), f32),
            block, block, block, block,
            pltpu.VMEM((rows, 2 * MODES), f32),
            pltpu.VMEM(response.shape, f32), pltpu.VMEM(mask.shape, jnp.int32),
        ] + [pltpu.VMEM(t.shape, bf16) for t in tables] + [
            dma((11,)), dma((12 + rad,)), dma((12 + rad,)), dma((2 * lat,)), dma((2 * lat,)), dma((shells,)),
        ],
        compiler_params=pltpu.CompilerParams(
            collective_id=0, has_side_effects=True, vmem_limit_bytes=60 * 1024 * 1024),
    )(disp, force, visc, layer, response, mask, *[jnp.asarray(t) for t in tables])


def solution(mesh):
    in_specs = (
        P("member", "radial", "lateral", None),
        P("member", "radial", "lateral", None),
        P("member"),
        P("radial", "lateral", None),
        P(None, "lateral"),
        P("lateral", None),
    )
    out_specs = (
        P("member", "radial", "lateral", None),
        P("member", ("lateral", "radial")),
        P("lateral", "member"),
    )
    body = functools.partial(shards, mesh.shape["lateral"], mesh.shape["radial"])
    return jax.shard_map(body, mesh=mesh, in_specs=in_specs, out_specs=out_specs, check_vma=False)
```

```python
import functools
import math

import jax
import jax.numpy as jnp
import ml_dtypes
import numpy as np
from jax import lax
from jax.experimental import pallas as pl
from jax.experimental.pallas import tpu as pltpu
from jax.sharding import PartitionSpec as P

MODES = 512
PAD = 8
VMEM = 67043328
MESH = pl.DeviceIdType.MESH
f32, bf16 = jnp.float32, jnp.bfloat16


def halves(table):
    table = table.astype(np.float32)
    high = table.astype(ml_dtypes.bfloat16)
    low = (table - high.astype(np.float32)).astype(ml_dtypes.bfloat16)
    return high, low


def longitude_quarter(count, modes):
    points = np.arange(count // 4)[:, None]
    phase = points * np.arange(modes)[None, :] % count
    angle = 2.0 * math.pi / count * phase
    table = np.concatenate([np.cos(angle), np.sin(angle)], axis=1)
    return halves(table * math.sqrt(2.0 / count))


def colatitude_table(count, modes):
    points = np.arange(count)[:, None]
    phase = np.arange(modes)[None, :] * (2 * points + 1) % (4 * count)
    table = np.cos(math.pi / (2 * count) * phase) * math.sqrt(2.0 / count)
    return halves(table)


def split(x):
    high = x.astype(bf16)
    return high, (x - high.astype(f32)).astype(bf16)


def dot(a, b, dims=(((1,), (0,)), ((), ()))):
    return lax.dot_general(a, b, dims, preferred_element_type=f32)


def choose(index, values):
    bit = 0
    while len(values) > 1:
        odd = (index & (1 << bit)) != 0
        values = [
            jnp.where(odd, values[min(i + 1, len(values) - 1)], values[i])
            for i in range(0, len(values), 2)
        ]
        bit += 1
    return values[0]


def kernel(lat, rad, layers, disp, force, visc, layer, response, mask, th, tl, ch, cl, cth, ctl,
           out, coef_out, sea_out,
           u0, u1, fv, li, he, r_out, r_in, e_out, e_in, l_out, l_in, surf, fsend, frecv, gsend, grecv, gather,
           resp_v, mask_v, th_v, tl_v, ch_v, cl_v, cth_v, ctl_v,
           load_sem, send_sem, recv_sem, a_send, a_recv):
    comps, shells, rows, lon = disp.shape
    width = response.shape[1]
    me = lax.axis_index("lateral")
    place = lax.axis_index("radial")
    inner = pl.ds(PAD, rows)

    def load(source, target, index):
        copy = pltpu.make_async_copy(source, target, load_sem.at[index])
        copy.start()
        return copy

    c_layer = load(layer, li.at[pl.ds(1, shells)], 0)
    c_disp = load(disp, u0.at[:, pl.ds(1, shells), inner], 1)
    c_force = load(force, fv, 2)
    pairs = [(response, resp_v), (mask, mask_v), (th, th_v), (tl, tl_v), (ch, ch_v), (cl, cl_v),
             (cth, cth_v), (ctl, ctl_v)]
    c_tables = [load(a, b, 3 + i) for i, (a, b) in enumerate(pairs)]

    barrier = pltpu.get_barrier_semaphore()
    for d in range(1, lat):
        pl.semaphore_signal(barrier, inc=1, device_id={"lateral": lax.rem(me + d, lat)}, device_id_type=MESH)
    for d in range(1, rad):
        pl.semaphore_signal(barrier, inc=1, device_id={"radial": lax.rem(place + d, rad)}, device_id_type=MESH)
    pl.semaphore_wait(barrier, lat + rad - 2)

    def remote(source, target, sem, axis, where):
        return pltpu.make_async_remote_copy(
            src_ref=source, dst_ref=target, send_sem=send_sem.at[sem], recv_sem=recv_sem.at[sem],
            device_id={axis: where}, device_id_type=MESH)

    above, below = place < rad - 1, place > 0
    south, north = me < lat - 1, me > 0
    up_id, down_id = lax.rem(place + 1, rad), lax.rem(place + rad - 1, rad)
    south_id, north_id = lax.rem(me + 1, lat), lax.rem(me + lat - 1, lat)

    li_up = remote(layer.at[shells - 1], li.at[0], 0, "radial", up_id)
    li_down = remote(layer.at[0], li.at[shells + 1], 1, "radial", down_id)
    d_up = remote(disp.at[:, shells - 1], u0.at[:, 0, inner], 2, "radial", up_id)
    d_down = remote(disp.at[:, 0], u0.at[:, shells + 1, inner], 3, "radial", down_id)

    @pl.when(above)
    def _():
        li_up.start()
        d_up.start()

    @pl.when(below)
    def _():
        li_down.start()
        d_down.start()

    values = [visc[i] * 0.5 for i in range(layers)]

    def lookup(s):
        for r in range(0, rows, 8):
            he[s, PAD + r:PAD + r + 8, :] = choose(li[s, r:r + 8, :], values)

    def lookup_step(i, carry):
        lookup(i + 1)
        return carry

    def stage(field, side, row):
        for c in range(comps):
            for s in range(shells):
                r_out[side, c * shells + s, :] = field[c, s + 1, PAD + row, :]

    def unstage(field, side, row):
        for c in range(comps):
            for s in range(shells):
                field[c, s + 1, row, :] = r_in[side, c * shells + s, :]

    def unstage_zero(field, row):
        for c in range(comps):
            for s in range(shells):
                field[c, s + 1, row, :] = jnp.zeros((lon,), f32)

    c_disp.wait()
    stage(u0, 0, rows - 1)
    stage(u0, 1, 0)
    r_south = remote(r_out.at[0], r_in.at[0], 4, "lateral", south_id)
    r_north = remote(r_out.at[1], r_in.at[1], 5, "lateral", north_id)

    @pl.when(south)
    def _():
        r_south.start()

    @pl.when(north)
    def _():
        r_north.start()

    c_layer.wait()
    lax.fori_loop(0, shells, lookup_step, 0)
    for s in range(shells):
        e_out[0, s, :] = he[s + 1, PAD + rows - 1, :]
        e_out[1, s, :] = he[s + 1, PAD, :]
    e_south = remote(e_out.at[0], e_in.at[0], 6, "lateral", south_id)
    e_north = remote(e_out.at[1], e_in.at[1], 7, "lateral", north_id)

    @pl.when(south)
    def _():
        e_south.start()

    @pl.when(north)
    def _():
        e_north.start()

    @pl.when(below)
    def _():
        li_up.wait_recv()
        lookup(0)
        d_up.wait_recv()

    @pl.when(jnp.logical_not(below))
    def _():
        he[0, PAD:PAD + rows, :] = jnp.zeros((rows, lon), f32)
        for c in range(comps):
            u0[c, 0, PAD:PAD + rows, :] = jnp.zeros((rows, lon), f32)
            u1[c, 0, PAD:PAD + rows, :] = jnp.zeros((rows, lon), f32)

    @pl.when(above)
    def _():
        li_down.wait_recv()
        lookup(shells + 1)
        d_down.wait_recv()

    @pl.when(jnp.logical_not(above))
    def _():
        he[shells + 1, PAD:PAD + rows, :] = jnp.zeros((rows, lon), f32)
        for c in range(comps):
            u0[c, shells + 1, PAD:PAD + rows, :] = jnp.zeros((rows, lon), f32)
            u1[c, shells + 1, PAD:PAD + rows, :] = jnp.zeros((rows, lon), f32)

    @pl.when(north)
    def _():
        r_south.wait_recv()
        e_south.wait_recv()
        unstage(u0, 0, PAD - 1)
        for s in range(shells):
            he[s + 1, PAD - 1, :] = e_in[0, s, :]

    @pl.when(jnp.logical_not(north))
    def _():
        unstage_zero(u0, PAD - 1)
        unstage_zero(u1, PAD - 1)
        for s in range(shells):
            he[s + 1, PAD - 1, :] = jnp.zeros((lon,), f32)

    @pl.when(south)
    def _():
        r_north.wait_recv()
        e_north.wait_recv()
        unstage(u0, 1, PAD + rows)
        for s in range(shells):
            he[s + 1, PAD + rows, :] = e_in[1, s, :]

    @pl.when(jnp.logical_not(south))
    def _():
        unstage_zero(u0, PAD + rows)
        unstage_zero(u1, PAD + rows)
        for s in range(shells):
            he[s + 1, PAD + rows, :] = jnp.zeros((lon,), f32)

    def sweep_shell(src, dst, s, lift=1, pad=PAD):
        for r in range(PAD, PAD + rows, 8):
            h = he[s + 1, r:r + 8, :]
            ws = [
                h + he[s + 2, r:r + 8, :],
                h + he[s, r:r + 8, :],
                h + he[s + 1, r + 1:r + 9, :],
                h + he[s + 1, r - 1:r + 7, :],
                h + pltpu.roll(h, 1, 1),
                h + pltpu.roll(h, lon - 1, 1),
            ]
            rate = 0.8 / (1.0 + (((ws[0] + ws[1]) + (ws[2] + ws[3])) + (ws[4] + ws[5])))
            for c in range(comps):
                u = src[c, s + 1, r:r + 8, :]
                total = fv[c, s, r - PAD:r - PAD + 8, :]
                total = total + ws[0] * src[c, s + 2, r:r + 8, :]
                total = total + ws[1] * src[c, s, r:r + 8, :]
                total = total + ws[2] * src[c, s + 1, r + 1:r + 9, :]
                total = total + ws[3] * src[c, s + 1, r - 1:r + 7, :]
                total = total + ws[4] * pltpu.roll(u, 1, 1)
                total = total + ws[5] * pltpu.roll(u, lon - 1, 1)
                dst[c, s + lift, r - PAD + pad:r - PAD + pad + 8, :] = 0.2 * u + rate * total

    c_force.wait()

    def first(i, carry):
        sweep_shell(u0, u1, i)
        return carry

    lax.fori_loop(0, shells, first, 0)

    @pl.when(above)
    def _():
        li_up.wait_send()
        d_up.wait_send()

    @pl.when(below)
    def _():
        li_down.wait_send()
        d_down.wait_send()

    @pl.when(south)
    def _():
        r_south.wait_send()
        e_south.wait_send()

    @pl.when(north)
    def _():
        r_north.wait_send()
        e_north.wait_send()

    g_up = remote(u1.at[:, shells, inner], u1.at[:, 0, inner], 8, "radial", up_id)
    g_down = remote(u1.at[:, 1, inner], u1.at[:, shells + 1, inner], 9, "radial", down_id)

    def stage_later(side, row):
        for c in range(comps):
            for s in range(shells):
                l_out[side, c * shells + s, :] = u1[c, s + 1, PAD + row, :]

    def unstage_later(side, row):
        for c in range(comps):
            for s in range(shells):
                u1[c, s + 1, row, :] = l_in[side, c * shells + s, :]

    s_south = remote(l_out.at[0], l_in.at[0], 10, "lateral", south_id)
    s_north = remote(l_out.at[1], l_in.at[1], 11, "lateral", north_id)
    stage_later(0, rows - 1)
    stage_later(1, 0)

    @pl.when(south)
    def _():
        s_south.start()

    @pl.when(north)
    def _():
        s_north.start()

    @pl.when(above)
    def _():
        g_up.start()

    @pl.when(below)
    def _():
        g_down.start()

    @pl.when(north)
    def _():
        s_south.wait_recv()
        unstage_later(0, PAD - 1)

    @pl.when(south)
    def _():
        s_north.wait_recv()
        unstage_later(1, PAD + rows)

    @pl.when(below)
    def _():
        g_up.wait_recv()

    @pl.when(above)
    def _():
        g_down.wait_recv()

    last = shells - 1
    sweep_shell(u1, out, last, 0, 0)

    top = place == rad - 1
    others = [
        remote(surf, surf, 12 + d - 1, "radial", lax.rem(place + d, rad)) for d in range(1, rad)
    ]

    @pl.when(top)
    def _():
        surf[...] = out[0, last]
        for copy in others:
            copy.start()

    def second(i, carry):
        sweep_shell(u1, out, i, 0, 0)
        return carry

    lax.fori_loop(0, 1, second, 0)

    for d in range(1, rad):
        @pl.when(place == d - 1)
        def _(d=d):
            others[rad - d - 1].wait_recv()

    for copy in c_tables:
        copy.wait()

    quarter = lon // 4
    modes = th.shape[1] // 2
    x = jnp.concatenate([surf[:, quarter * m:quarter * (m + 1)] for m in range(4)], axis=0)
    xh, xl = split(x)
    g = dot(xh, th_v[...]) + dot(xl, th_v[...]) + dot(xh, tl_v[...])
    gc = [g[rows * m:rows * (m + 1), :modes] for m in range(4)]
    gs = [g[rows * m:rows * (m + 1), modes:] for m in range(4)]
    wave = lax.broadcasted_iota(jnp.int32, (rows, modes), 1) & 3
    zero, one = jnp.zeros((rows, modes), f32), jnp.ones((rows, modes), f32)
    e1 = jnp.where(wave == 0, one, jnp.where(wave == 2, -one, zero))
    s1 = jnp.where(wave == 1, one, jnp.where(wave == 3, -one, zero))
    e2 = jnp.where((wave & 1) == 0, one, -one)
    fc = gc[0] + e2 * gc[2] + e1 * (gc[1] + gc[3]) - s1 * (gs[1] - gs[3])
    fs = gs[0] + e2 * gs[2] + e1 * (gs[1] + gs[3]) + s1 * (gc[1] - gc[3])
    fourier = jnp.concatenate([fc, fs], axis=1)
    for p in range(lat):
        fsend[p] = fourier[:, p * width:(p + 1) * width]

    def exchange(source, target, base):
        copies = []
        for d in range(1, lat):
            peer = lax.rem(me + d, lat)
            copies.append(pltpu.make_async_remote_copy(
                src_ref=source.at[peer], dst_ref=target.at[me],
                send_sem=a_send.at[base + d], recv_sem=a_recv.at[base + d],
                device_id={"lateral": peer}, device_id_type=MESH))
        for copy in copies:
            copy.start()
        return copies

    copies_f = exchange(fsend, frecv, 0)
    frecv[me] = fsend[me]
    lax.fori_loop(1, shells - 1, second, 0)
    for copy in copies_f:
        copy.wait()

    field = frecv[...].reshape(lat * rows, width)
    fh, fl = split(field)
    coef = dot(cth_v[...], fh) + dot(cth_v[...], fl) + dot(ctl_v[...], fh)
    half = width // rad
    for r in range(rad):
        @pl.when(place == r)
        def _(r=r):
            coef_out[...] = coef[:, r * half:(r + 1) * half].T
    sh, sl = split(resp_v[...] * coef)
    load_rows = dot(ch_v[...], sh) + dot(ch_v[...], sl) + dot(cl_v[...], sh)
    gsend[...] = load_rows.reshape(lat, rows, width)
    copies_g = exchange(gsend, grecv, lat)
    grecv[me] = gsend[me]
    for copy in copies_g:
        copy.wait()
    for p in range(lat):
        gather[:, p * width:(p + 1) * width] = grecv[p]
    rc, rs = gather[:, :modes], gather[:, modes:]
    twisted = [
        (rc, rs),
        (e1 * rc + s1 * rs, e1 * rs - s1 * rc),
        (e2 * rc, e2 * rs),
        (e1 * rc - s1 * rs, e1 * rs + s1 * rc),
    ]
    a = jnp.concatenate([jnp.concatenate(pair, axis=1) for pair in twisted], axis=0)
    ah, al = split(a)
    nt = (((1,), (1,)), ((), ()))
    sea = dot(ah, th_v[...], nt) + dot(al, th_v[...], nt) + dot(ah, tl_v[...], nt)
    for m in range(4):
        cut = slice(quarter * m, quarter * (m + 1))
        sea_out[:, cut] = mask_v[:, cut].astype(f32) * sea[rows * m:rows * (m + 1)]

    @pl.when(south)
    def _():
        s_south.wait_send()

    @pl.when(north)
    def _():
        s_north.wait_send()

    @pl.when(above)
    def _():
        g_up.wait_send()

    @pl.when(below)
    def _():
        g_down.wait_send()

    @pl.when(top)
    def _():
        for copy in others:
            copy.wait_send()


def shards(lat, rad, disp, force, visc, layer, response, mask):
    comps, shells, rows, lon = disp.shape
    width = response.shape[1]
    th, tl = longitude_quarter(lon, MODES)
    ch, cl = colatitude_table(lat * rows, MODES)
    tables = [th, tl, ch, cl, ch.T.copy(), cl.T.copy()]
    hbm = pl.BlockSpec(memory_space=pltpu.HBM)
    vmem = pl.BlockSpec(memory_space=pltpu.VMEM)
    field = pltpu.VMEM((comps, shells + 2, rows + 2 * PAD, lon), f32)
    staged = [pltpu.VMEM((2, n, lon), f32) for n in (comps * shells, shells, comps * shells) for _ in range(2)]
    block = pltpu.VMEM((lat, rows, width), f32)
    dma = pltpu.SemaphoreType.DMA
    spare = 4 * (disp.size + MODES * width // rad + rows * lon) + 65536
    out, coef, sea = pl.pallas_call(
        functools.partial(kernel, lat, rad, visc.shape[0]),
        out_shape=(
            pltpu.VMEM(disp.shape, f32),
            pltpu.VMEM((width // rad, MODES), f32),
            pltpu.VMEM((rows, lon), f32),
        ),
        in_specs=[hbm, hbm, pl.BlockSpec(memory_space=pltpu.SMEM)] + [hbm] * 9,
        out_specs=(vmem, vmem, vmem),
        scratch_shapes=[
            field, field,
            pltpu.VMEM((comps, shells, rows, lon), f32),
            pltpu.VMEM((shells + 2, rows, lon), jnp.int32),
            pltpu.VMEM((shells + 2, rows + 2 * PAD, lon), f32),
            *staged,
            pltpu.VMEM((rows, lon), f32),
            block, block, block, block,
            pltpu.VMEM((rows, 2 * MODES), f32),
            pltpu.VMEM(response.shape, f32), pltpu.VMEM(mask.shape, jnp.int32),
        ] + [pltpu.VMEM(t.shape, bf16) for t in tables] + [
            dma((11,)), dma((12 + rad,)), dma((12 + rad,)), dma((2 * lat,)), dma((2 * lat,)),
        ],
        compiler_params=pltpu.CompilerParams(
            collective_id=0, has_side_effects=True, vmem_limit_bytes=VMEM - spare),
    )(disp, force, visc, layer, response, mask, *[jnp.asarray(t) for t in tables])
    return out, coef.T, sea


def solution(mesh):
    in_specs = (
        P("member", "radial", "lateral", None),
        P("member", "radial", "lateral", None),
        P("member"),
        P("radial", "lateral", None),
        P(None, "lateral"),
        P("lateral", None),
    )
    out_specs = (
        P("member", "radial", "lateral", None),
        P("member", ("lateral", "radial")),
        P("lateral", "member"),
    )
    body = functools.partial(shards, mesh.shape["lateral"], mesh.shape["radial"])
    return jax.shard_map(body, mesh=mesh, in_specs=in_specs, out_specs=out_specs, check_vma=False)
```

```python
import functools
import math

import jax
import jax.numpy as jnp
import ml_dtypes
import numpy as np
from jax import lax
from jax.experimental import pallas as pl
from jax.experimental.pallas import tpu as pltpu
from jax.sharding import PartitionSpec as P

MODES = 512
PAD = 8
VMEM = 67043328
MESH = pl.DeviceIdType.MESH
f32, bf16 = jnp.float32, jnp.bfloat16


def halves(table):
    table = table.astype(np.float32)
    high = table.astype(ml_dtypes.bfloat16)
    low = (table - high.astype(np.float32)).astype(ml_dtypes.bfloat16)
    return high, low


def longitude_quarter(count, modes):
    points = np.arange(count // 4)[:, None]
    phase = points * np.arange(modes)[None, :] % count
    angle = 2.0 * math.pi / count * phase
    table = np.concatenate([np.cos(angle), np.sin(angle)], axis=1)
    return halves(table * math.sqrt(2.0 / count))


def colatitude_table(count, modes):
    points = np.arange(count)[:, None]
    phase = np.arange(modes)[None, :] * (2 * points + 1) % (4 * count)
    table = np.cos(math.pi / (2 * count) * phase) * math.sqrt(2.0 / count)
    return halves(table)


def split(x):
    high = x.astype(bf16)
    return high, (x - high.astype(f32)).astype(bf16)


def dot(a, b, dims=(((1,), (0,)), ((), ()))):
    return lax.dot_general(a, b, dims, preferred_element_type=f32)


def choose(index, values):
    bit = 0
    while len(values) > 1:
        odd = (index & (1 << bit)) != 0
        values = [
            jnp.where(odd, values[min(i + 1, len(values) - 1)], values[i])
            for i in range(0, len(values), 2)
        ]
        bit += 1
    return values[0]


def kernel(lat, rad, layers, disp, force, visc, layer, response, mask, th, tl, ch, cl, cth, ctl,
           out, coef_out, sea_out,
           u0, u1, fv, li, he, r_out, r_in, e_out, e_in, l_out, l_in, fsend, frecv, gsend, grecv, gather,
           resp_v, mask_v, th_v, tl_v, ch_v, cl_v, cth_v, ctl_v,
           load_sem, send_sem, recv_sem, a_send, a_recv, b_send, b_recv):
    comps, shells, rows, lon = disp.shape
    width = response.shape[1]
    me = lax.axis_index("lateral")
    place = lax.axis_index("radial")
    inner = pl.ds(PAD, rows)

    def load(source, target, index):
        copy = pltpu.make_async_copy(source, target, load_sem.at[index])
        copy.start()
        return copy

    c_layer = load(layer, li.at[pl.ds(1, shells)], 0)
    c_disp = load(disp, u0.at[:, pl.ds(1, shells), inner], 1)
    c_force = load(force, fv, 2)
    pairs = [(response, resp_v), (mask, mask_v), (th, th_v), (tl, tl_v), (ch, ch_v), (cl, cl_v),
             (cth, cth_v), (ctl, ctl_v)]
    def around(d, e):
        return {"lateral": lax.rem(me + d, lat), "radial": lax.rem(place + e, rad)}

    barrier = pltpu.get_barrier_semaphore()
    offsets = [(d, e) for d in range(lat) for e in range(rad) if d or e]
    for d, e in offsets:
        pl.semaphore_signal(barrier, inc=1, device_id=around(d, e), device_id_type=MESH)
    pl.semaphore_wait(barrier, lat * rad - 1)

    def remote(source, target, sem, axis, where):
        return pltpu.make_async_remote_copy(
            src_ref=source, dst_ref=target, send_sem=send_sem.at[sem], recv_sem=recv_sem.at[sem],
            device_id={axis: where}, device_id_type=MESH)

    above, below = place < rad - 1, place > 0
    south, north = me < lat - 1, me > 0
    up_id, down_id = lax.rem(place + 1, rad), lax.rem(place + rad - 1, rad)
    south_id, north_id = lax.rem(me + 1, lat), lax.rem(me + lat - 1, lat)

    li_up = remote(layer.at[shells - 1], li.at[0], 0, "radial", up_id)
    li_down = remote(layer.at[0], li.at[shells + 1], 1, "radial", down_id)
    d_up = remote(disp.at[:, shells - 1], u0.at[:, 0, inner], 2, "radial", up_id)
    d_down = remote(disp.at[:, 0], u0.at[:, shells + 1, inner], 3, "radial", down_id)

    @pl.when(above)
    def _():
        li_up.start()
        d_up.start()

    @pl.when(below)
    def _():
        li_down.start()
        d_down.start()

    values = [visc[i] * 0.5 for i in range(layers)]

    def lookup(s):
        for r in range(0, rows, 8):
            he[s, PAD + r:PAD + r + 8, :] = choose(li[s, r:r + 8, :], values)

    def lookup_step(i, carry):
        lookup(i + 1)
        return carry

    def stage(field, side, row):
        for c in range(comps):
            for s in range(shells):
                r_out[side, c * shells + s, :] = field[c, s + 1, PAD + row, :]

    def unstage(field, side, row):
        for c in range(comps):
            for s in range(shells):
                field[c, s + 1, row, :] = r_in[side, c * shells + s, :]

    def unstage_zero(field, row):
        for c in range(comps):
            for s in range(shells):
                field[c, s + 1, row, :] = jnp.zeros((lon,), f32)

    c_disp.wait()
    c_tables = [load(a, b, 3 + i) for i, (a, b) in enumerate(pairs)]
    stage(u0, 0, rows - 1)
    stage(u0, 1, 0)
    r_south = remote(r_out.at[0], r_in.at[0], 4, "lateral", south_id)
    r_north = remote(r_out.at[1], r_in.at[1], 5, "lateral", north_id)

    @pl.when(south)
    def _():
        r_south.start()

    @pl.when(north)
    def _():
        r_north.start()

    c_layer.wait()
    lax.fori_loop(0, shells, lookup_step, 0)
    for s in range(shells):
        e_out[0, s, :] = he[s + 1, PAD + rows - 1, :]
        e_out[1, s, :] = he[s + 1, PAD, :]
    e_south = remote(e_out.at[0], e_in.at[0], 6, "lateral", south_id)
    e_north = remote(e_out.at[1], e_in.at[1], 7, "lateral", north_id)

    @pl.when(south)
    def _():
        e_south.start()

    @pl.when(north)
    def _():
        e_north.start()

    @pl.when(below)
    def _():
        li_up.wait_recv()
        lookup(0)
        d_up.wait_recv()

    @pl.when(jnp.logical_not(below))
    def _():
        he[0, PAD:PAD + rows, :] = jnp.zeros((rows, lon), f32)
        for c in range(comps):
            u0[c, 0, PAD:PAD + rows, :] = jnp.zeros((rows, lon), f32)
            u1[c, 0, PAD:PAD + rows, :] = jnp.zeros((rows, lon), f32)

    @pl.when(above)
    def _():
        li_down.wait_recv()
        lookup(shells + 1)
        d_down.wait_recv()

    @pl.when(jnp.logical_not(above))
    def _():
        he[shells + 1, PAD:PAD + rows, :] = jnp.zeros((rows, lon), f32)
        for c in range(comps):
            u0[c, shells + 1, PAD:PAD + rows, :] = jnp.zeros((rows, lon), f32)
            u1[c, shells + 1, PAD:PAD + rows, :] = jnp.zeros((rows, lon), f32)

    @pl.when(north)
    def _():
        r_south.wait_recv()
        e_south.wait_recv()
        unstage(u0, 0, PAD - 1)
        for s in range(shells):
            he[s + 1, PAD - 1, :] = e_in[0, s, :]

    @pl.when(jnp.logical_not(north))
    def _():
        unstage_zero(u0, PAD - 1)
        unstage_zero(u1, PAD - 1)
        for s in range(shells):
            he[s + 1, PAD - 1, :] = jnp.zeros((lon,), f32)

    @pl.when(south)
    def _():
        r_north.wait_recv()
        e_north.wait_recv()
        unstage(u0, 1, PAD + rows)
        for s in range(shells):
            he[s + 1, PAD + rows, :] = e_in[1, s, :]

    @pl.when(jnp.logical_not(south))
    def _():
        unstage_zero(u0, PAD + rows)
        unstage_zero(u1, PAD + rows)
        for s in range(shells):
            he[s + 1, PAD + rows, :] = jnp.zeros((lon,), f32)

    chunk = lon // 4

    def beside(load, k):
        first, end = k * chunk, (k + 1) * chunk
        mid = load(slice(first, end))
        before = load(slice((first - 128) % lon, (first - 128) % lon + 128))
        after = load(slice(end % lon, end % lon + 128))
        left = pltpu.roll(jnp.concatenate([before, mid], axis=1), 1, 1)[:, 128:]
        right = pltpu.roll(jnp.concatenate([mid, after], axis=1), chunk + 127, 1)[:, :chunk]
        return mid, left, right

    def sweep_block(src, dst, s, r, lift, pad):
        r = r + PAD
        here, next_row, last_row = slice(r, r + 8), slice(r + 1, r + 9), slice(r - 1, r + 7)
        for k in range(4):
            lanes = slice(k * chunk, (k + 1) * chunk)
            h, left, right = beside(lambda cols: he[s + 1, here, cols], k)
            ws = [
                h + he[s + 2, here, lanes],
                h + he[s, here, lanes],
                h + he[s + 1, next_row, lanes],
                h + he[s + 1, last_row, lanes],
                h + left,
                h + right,
            ]
            rate = 0.8 / (1.0 + (((ws[0] + ws[1]) + (ws[2] + ws[3])) + (ws[4] + ws[5])))
            for c in range(comps):
                u, left, right = beside(lambda cols: src[c, s + 1, here, cols], k)
                total = fv[c, s, r - PAD:r - PAD + 8, lanes]
                total = total + ws[0] * src[c, s + 2, here, lanes]
                total = total + ws[1] * src[c, s, here, lanes]
                total = total + ws[2] * src[c, s + 1, next_row, lanes]
                total = total + ws[3] * src[c, s + 1, last_row, lanes]
                total = total + ws[4] * left
                total = total + ws[5] * right
                dst[c, s + lift, r - PAD + pad:r - PAD + pad + 8, lanes] = 0.2 * u + rate * total

    c_force.wait()

    edge_rows = sorted({0, rows - 8})
    inner_rows = list(range(8, rows - 8, 8))

    def edges(s, carry):
        for r in edge_rows:
            sweep_block(u0, u1, s, r, 1, PAD)
        return carry

    lax.fori_loop(0, shells, edges, 0)

    @pl.when(above)
    def _():
        li_up.wait_send()
        d_up.wait_send()

    @pl.when(below)
    def _():
        li_down.wait_send()
        d_down.wait_send()

    @pl.when(south)
    def _():
        r_south.wait_send()
        e_south.wait_send()

    @pl.when(north)
    def _():
        r_north.wait_send()
        e_north.wait_send()

    g_up = remote(u1.at[:, shells, inner], u1.at[:, 0, inner], 8, "radial", up_id)
    g_down = remote(u1.at[:, 1, inner], u1.at[:, shells + 1, inner], 9, "radial", down_id)

    def stage_later(side, row):
        for c in range(comps):
            for s in range(shells):
                l_out[side, c * shells + s, :] = u1[c, s + 1, PAD + row, :]

    def unstage_later(side, row):
        for c in range(comps):
            for s in range(shells):
                u1[c, s + 1, row, :] = l_in[side, c * shells + s, :]

    s_south = remote(l_out.at[0], l_in.at[0], 10, "lateral", south_id)
    s_north = remote(l_out.at[1], l_in.at[1], 11, "lateral", north_id)
    stage_later(0, rows - 1)
    stage_later(1, 0)

    @pl.when(south)
    def _():
        s_south.start()

    @pl.when(north)
    def _():
        s_north.start()

    def insides(i, carry):
        s = i + jnp.where(above, 1, 0) * (shells - 1 - 2 * i)
        for r in inner_rows:
            sweep_block(u0, u1, s, r, 1, PAD)

        @pl.when(jnp.logical_and(above, s == shells - 1))
        def _():
            g_up.start()

        @pl.when(jnp.logical_and(below, s == 0))
        def _():
            g_down.start()

        return carry

    lax.fori_loop(0, shells, insides, 0)

    @pl.when(north)
    def _():
        s_south.wait_recv()
        unstage_later(0, PAD - 1)

    @pl.when(south)
    def _():
        s_north.wait_recv()
        unstage_later(1, PAD + rows)

    @pl.when(below)
    def _():
        g_up.wait_recv()

    @pl.when(above)
    def _():
        g_down.wait_recv()

    last = shells - 1
    top = place == rad - 1

    def second(s, carry):
        for r in range(0, rows, 8):
            sweep_block(u1, out, s, r, 0, 0)
        return carry

    second(last, 0)
    for copy in c_tables:
        copy.wait()

    quarter = lon // 4
    modes = th.shape[1] // 2
    wave = lax.broadcasted_iota(jnp.int32, (rows, modes), 1) & 3
    zero, one = jnp.zeros((rows, modes), f32), jnp.ones((rows, modes), f32)
    e1 = jnp.where(wave == 0, one, jnp.where(wave == 2, -one, zero))
    s1 = jnp.where(wave == 1, one, jnp.where(wave == 3, -one, zero))
    e2 = jnp.where((wave & 1) == 0, one, -one)
    half = width // rad
    forward = []
    for d, e in [(d, e) for d in range(lat) for e in range(rad) if d or e != rad - 1]:
        peer = lax.rem(me + d, lat)
        forward.append((d, e, pltpu.make_async_remote_copy(
            src_ref=fsend.at[peer, e], dst_ref=frecv.at[me],
            send_sem=a_send.at[d * rad + e], recv_sem=a_recv.at[d],
            device_id={"lateral": peer, "radial": e}, device_id_type=MESH)))

    @pl.when(top)
    def _():
        x = jnp.concatenate([out[0, last, :, quarter * m:quarter * (m + 1)] for m in range(4)], axis=0)
        xh, xl = split(x)
        g = dot(xh, th_v[...]) + dot(xl, th_v[...]) + dot(xh, tl_v[...])
        gc = [g[rows * m:rows * (m + 1), :modes] for m in range(4)]
        gs = [g[rows * m:rows * (m + 1), modes:] for m in range(4)]
        fc = gc[0] + e2 * gc[2] + e1 * (gc[1] + gc[3]) - s1 * (gs[1] - gs[3])
        fs = gs[0] + e2 * gs[2] + e1 * (gs[1] + gs[3]) + s1 * (gc[1] - gc[3])
        fourier = jnp.concatenate([fc, fs], axis=1)
        for p in range(lat):
            for e in range(rad):
                fsend[p, e] = fourier[:, p * width + e * half:p * width + (e + 1) * half]
        for _, _, copy in forward:
            copy.start()
        frecv[me] = fsend[me, rad - 1]

    lax.fori_loop(0, last, second, 0)

    @pl.when(top)
    def _():
        for d, e, copy in forward:
            if e == rad - 1:
                copy.wait_recv()
        for _, _, copy in forward:
            copy.wait_send()

    @pl.when(jnp.logical_not(top))
    def _():
        for d, e, copy in forward:
            if e == 0:
                copy.wait_recv()

    field = frecv[...].reshape(lat * rows, half)
    fh, fl = split(field)
    coef = dot(cth_v[...], fh) + dot(cth_v[...], fl) + dot(ctl_v[...], fh)
    answer = resp_v[:, :half]
    for e in range(1, rad):
        answer = jnp.where(place == e, resp_v[:, e * half:(e + 1) * half], answer)
    sh, sl = split(answer * coef)
    load_rows = dot(ch_v[...], sh) + dot(ch_v[...], sl) + dot(cl_v[...], sh)
    gsend[...] = load_rows.reshape(lat, rows, half)
    back = []
    for d, e in offsets:
        back.append(pltpu.make_async_remote_copy(
            src_ref=gsend.at[lax.rem(me + d, lat)], dst_ref=grecv.at[me, place],
            send_sem=b_send.at[d * rad + e], recv_sem=b_recv.at[d * rad + e],
            device_id=around(d, e), device_id_type=MESH))
    for copy in back:
        copy.start()
    grecv[me, place] = gsend[me]
    coef_out[...] = coef.T
    for copy in back:
        copy.wait()
    for p in range(lat):
        for e in range(rad):
            gather[:, p * width + e * half:p * width + (e + 1) * half] = grecv[p, e]
    rc, rs = gather[:, :modes], gather[:, modes:]
    twisted = [
        (rc, rs),
        (e1 * rc + s1 * rs, e1 * rs - s1 * rc),
        (e2 * rc, e2 * rs),
        (e1 * rc - s1 * rs, e1 * rs + s1 * rc),
    ]
    a = jnp.concatenate([jnp.concatenate(pair, axis=1) for pair in twisted], axis=0)
    ah, al = split(a)
    nt = (((1,), (1,)), ((), ()))
    sea = dot(ah, th_v[...], nt) + dot(al, th_v[...], nt) + dot(ah, tl_v[...], nt)
    for m in range(4):
        cut = slice(quarter * m, quarter * (m + 1))
        sea_out[:, cut] = mask_v[:, cut].astype(f32) * sea[rows * m:rows * (m + 1)]

    @pl.when(south)
    def _():
        s_south.wait_send()

    @pl.when(north)
    def _():
        s_north.wait_send()

    @pl.when(above)
    def _():
        g_up.wait_send()

    @pl.when(below)
    def _():
        g_down.wait_send()


def writer(a, b, c, a_out, b_out, c_out, sem):
    copies = [
        pltpu.make_async_copy(source, target, sem.at[i])
        for i, (source, target) in enumerate([(a, a_out), (b, b_out), (c, c_out)])
    ]
    for copy in copies:
        copy.start()
    for copy in copies:
        copy.wait()


def shards(lat, rad, disp, force, visc, layer, response, mask):
    comps, shells, rows, lon = disp.shape
    width = response.shape[1]
    th, tl = longitude_quarter(lon, MODES)
    ch, cl = colatitude_table(lat * rows, MODES)
    tables = [th, tl, ch, cl, ch.T.copy(), cl.T.copy()]
    hbm = pl.BlockSpec(memory_space=pltpu.HBM)
    vmem = pl.BlockSpec(memory_space=pltpu.VMEM)
    field = pltpu.VMEM((comps, shells + 2, rows + 2 * PAD, lon), f32)
    staged = [pltpu.VMEM((2, n, lon), f32) for n in (comps * shells, shells, comps * shells) for _ in range(2)]
    half = width // rad
    block = pltpu.VMEM((lat, rows, half), f32)
    dma = pltpu.SemaphoreType.DMA
    spare = 4 * (disp.size + MODES * width // rad + rows * lon) + 65536
    out, coef, sea = pl.pallas_call(
        functools.partial(kernel, lat, rad, visc.shape[0]),
        out_shape=(
            pltpu.VMEM(disp.shape, f32),
            pltpu.VMEM((width // rad, MODES), f32),
            pltpu.VMEM((rows, lon), f32),
        ),
        in_specs=[hbm, hbm, pl.BlockSpec(memory_space=pltpu.SMEM)] + [hbm] * 9,
        out_specs=(vmem, vmem, vmem),
        scratch_shapes=[
            field, field,
            pltpu.VMEM((comps, shells, rows, lon), f32),
            pltpu.VMEM((shells + 2, rows, lon), jnp.int32),
            pltpu.VMEM((shells + 2, rows + 2 * PAD, lon), f32),
            *staged,
            pltpu.VMEM((lat, rad, rows, half), f32), block, block, pltpu.VMEM((lat, rad, rows, half), f32),
            pltpu.VMEM((rows, 2 * MODES), f32),
            pltpu.VMEM(response.shape, f32), pltpu.VMEM(mask.shape, jnp.int32),
        ] + [pltpu.VMEM(t.shape, bf16) for t in tables] + [
            dma((11,)), dma((12,)), dma((12,)), dma((lat * rad,)), dma((lat,)),
            dma((lat * rad,)), dma((lat * rad,)),
        ],
        compiler_params=pltpu.CompilerParams(
            collective_id=0, has_side_effects=True, vmem_limit_bytes=VMEM - spare),
    )(disp, force, visc, layer, response, mask, *[jnp.asarray(t) for t in tables])
    out, coef, sea = pl.pallas_call(
        writer,
        out_shape=tuple(jax.ShapeDtypeStruct(a.shape, f32) for a in (out, coef, sea)),
        in_specs=[vmem] * 3,
        out_specs=(hbm, hbm, hbm),
        scratch_shapes=[dma((3,))],
        compiler_params=pltpu.CompilerParams(vmem_limit_bytes=1 << 20),
    )(out, coef, sea)
    return out, coef.T, sea


def solution(mesh):
    in_specs = (
        P("member", "radial", "lateral", None),
        P("member", "radial", "lateral", None),
        P("member"),
        P("radial", "lateral", None),
        P(None, "lateral"),
        P("lateral", None),
    )
    out_specs = (
        P("member", "radial", "lateral", None),
        P("member", ("lateral", "radial")),
        P("lateral", "member"),
    )
    body = functools.partial(shards, mesh.shape["lateral"], mesh.shape["radial"])
    return jax.shard_map(body, mesh=mesh, in_specs=in_specs, out_specs=out_specs, check_vma=False)
```

```python
import functools
import math

import jax
import jax.numpy as jnp
import ml_dtypes
import numpy as np
from jax import lax
from jax.experimental import pallas as pl
from jax.experimental.pallas import tpu as pltpu
from jax.sharding import PartitionSpec as P

MODES = 512
PAD = 8
VMEM = 67043328
MESH = pl.DeviceIdType.MESH
f32, bf16 = jnp.float32, jnp.bfloat16


def halves(table):
    table = table.astype(np.float32)
    high = table.astype(ml_dtypes.bfloat16)
    low = (table - high.astype(np.float32)).astype(ml_dtypes.bfloat16)
    return high, low


def longitude_quarter(count, modes):
    points = np.arange(count // 4)[:, None]
    phase = points * np.arange(modes)[None, :] % count
    angle = 2.0 * math.pi / count * phase
    table = np.concatenate([np.cos(angle), np.sin(angle)], axis=1)
    return halves(table * math.sqrt(2.0 / count))


def colatitude_table(count, modes):
    points = np.arange(count)[:, None]
    phase = np.arange(modes)[None, :] * (2 * points + 1) % (4 * count)
    table = np.cos(math.pi / (2 * count) * phase) * math.sqrt(2.0 / count)
    return halves(table)


def split(x):
    high = x.astype(bf16)
    return high, (x - high.astype(f32)).astype(bf16)


def dot(a, b, dims=(((1,), (0,)), ((), ()))):
    return lax.dot_general(a, b, dims, preferred_element_type=f32)


def choose(index, values):
    bit = 0
    while len(values) > 1:
        odd = (index & (1 << bit)) != 0
        values = [
            jnp.where(odd, values[min(i + 1, len(values) - 1)], values[i])
            for i in range(0, len(values), 2)
        ]
        bit += 1
    return values[0]


def kernel(lat, rad, layers, disp, force, visc, layer, response, mask, th, tl, ch, cl, cth, ctl,
           out, coef_out, sea_out,
           u0, u1, fv, li, he, r_out, r_in, e_out, e_in, l_out, l_in, fsend, frecv, gsend, grecv, gather,
           resp_v, mask_v, th_v, tl_v, ch_v, cl_v, cth_v, ctl_v,
           load_sem, send_sem, recv_sem, a_send, a_recv, b_send, b_recv):
    comps, shells, rows, lon = disp.shape
    width = response.shape[1]
    me = lax.axis_index("lateral")
    place = lax.axis_index("radial")
    inner = pl.ds(PAD, rows)

    def load(source, target, index):
        copy = pltpu.make_async_copy(source, target, load_sem.at[index])
        copy.start()
        return copy

    c_layer = load(layer, li, 0)
    c_disp = load(disp, u0.at[:, pl.ds(1, shells), inner], 1)
    c_force = load(force, fv, 2)
    pairs = [(response, resp_v), (mask, mask_v), (th, th_v), (tl, tl_v), (ch, ch_v), (cl, cl_v),
             (cth, cth_v), (ctl, ctl_v)]
    def around(d, e):
        return {"lateral": lax.rem(me + d, lat), "radial": lax.rem(place + e, rad)}

    barrier = pltpu.get_barrier_semaphore()
    offsets = [(d, e) for d in range(lat) for e in range(rad) if d or e]
    for d, e in offsets:
        pl.semaphore_signal(barrier, inc=1, device_id=around(d, e), device_id_type=MESH)

    def remote(source, target, sem, axis, where):
        return pltpu.make_async_remote_copy(
            src_ref=source, dst_ref=target, send_sem=send_sem.at[sem], recv_sem=recv_sem.at[sem],
            device_id={axis: where}, device_id_type=MESH)

    above, below = place < rad - 1, place > 0
    south, north = me < lat - 1, me > 0
    up_id, down_id = lax.rem(place + 1, rad), lax.rem(place + rad - 1, rad)
    south_id, north_id = lax.rem(me + 1, lat), lax.rem(me + lat - 1, lat)

    he_up = remote(he.at[shells, inner], he.at[0, inner], 0, "radial", up_id)
    he_down = remote(he.at[1, inner], he.at[shells + 1, inner], 1, "radial", down_id)
    d_up = remote(disp.at[:, shells - 1], u0.at[:, 0, inner], 2, "radial", up_id)
    d_down = remote(disp.at[:, 0], u0.at[:, shells + 1, inner], 3, "radial", down_id)

    values = [visc[i] * 0.5 for i in range(layers)]

    def lookup(s):
        for r in range(0, rows, 8):
            he[s, PAD + r:PAD + r + 8, :] = choose(li[s - 1, r:r + 8, :], values)

    def lookup_step(i, carry):
        lookup(i + 1)
        return carry

    def stage(field, side, row):
        for c in range(comps):
            for s in range(shells):
                r_out[side, c * shells + s, :] = field[c, s + 1, PAD + row, :]

    def unstage(field, side, row):
        for c in range(comps):
            for s in range(shells):
                field[c, s + 1, row, :] = r_in[side, c * shells + s, :]

    def unstage_zero(field, row):
        for c in range(comps):
            for s in range(shells):
                field[c, s + 1, row, :] = jnp.zeros((lon,), f32)

    c_disp.wait()
    c_tables = [load(a, b, 3 + i) for i, (a, b) in enumerate(pairs)]
    stage(u0, 0, rows - 1)
    stage(u0, 1, 0)
    r_south = remote(r_out.at[0], r_in.at[0], 4, "lateral", south_id)
    r_north = remote(r_out.at[1], r_in.at[1], 5, "lateral", north_id)

    c_layer.wait()
    lax.fori_loop(0, shells, lookup_step, 0)
    for s in range(shells):
        e_out[0, s, :] = he[s + 1, PAD + rows - 1, :]
        e_out[1, s, :] = he[s + 1, PAD, :]
    e_south = remote(e_out.at[0], e_in.at[0], 6, "lateral", south_id)
    e_north = remote(e_out.at[1], e_in.at[1], 7, "lateral", north_id)

    pl.semaphore_wait(barrier, lat * rad - 1)

    @pl.when(south)
    def _():
        r_south.start()
        e_south.start()

    @pl.when(north)
    def _():
        r_north.start()
        e_north.start()

    @pl.when(above)
    def _():
        he_up.start()
        d_up.start()

    @pl.when(below)
    def _():
        he_down.start()
        d_down.start()

    @pl.when(below)
    def _():
        he_up.wait_recv()
        d_up.wait_recv()

    @pl.when(jnp.logical_not(below))
    def _():
        he[0, PAD:PAD + rows, :] = jnp.zeros((rows, lon), f32)
        for c in range(comps):
            u0[c, 0, PAD:PAD + rows, :] = jnp.zeros((rows, lon), f32)
            u1[c, 0, PAD:PAD + rows, :] = jnp.zeros((rows, lon), f32)

    @pl.when(above)
    def _():
        he_down.wait_recv()
        d_down.wait_recv()

    @pl.when(jnp.logical_not(above))
    def _():
        he[shells + 1, PAD:PAD + rows, :] = jnp.zeros((rows, lon), f32)
        for c in range(comps):
            u0[c, shells + 1, PAD:PAD + rows, :] = jnp.zeros((rows, lon), f32)
            u1[c, shells + 1, PAD:PAD + rows, :] = jnp.zeros((rows, lon), f32)

    @pl.when(north)
    def _():
        r_south.wait_recv()
        e_south.wait_recv()
        unstage(u0, 0, PAD - 1)
        for s in range(shells):
            he[s + 1, PAD - 1, :] = e_in[0, s, :]

    @pl.when(jnp.logical_not(north))
    def _():
        unstage_zero(u0, PAD - 1)
        unstage_zero(u1, PAD - 1)
        for s in range(shells):
            he[s + 1, PAD - 1, :] = jnp.zeros((lon,), f32)

    @pl.when(south)
    def _():
        r_north.wait_recv()
        e_north.wait_recv()
        unstage(u0, 1, PAD + rows)
        for s in range(shells):
            he[s + 1, PAD + rows, :] = e_in[1, s, :]

    @pl.when(jnp.logical_not(south))
    def _():
        unstage_zero(u0, PAD + rows)
        unstage_zero(u1, PAD + rows)
        for s in range(shells):
            he[s + 1, PAD + rows, :] = jnp.zeros((lon,), f32)

    chunk = lon // 4

    def beside(load, k):
        first, end = k * chunk, (k + 1) * chunk
        mid = load(slice(first, end))
        before = load(slice((first - 128) % lon, (first - 128) % lon + 128))
        after = load(slice(end % lon, end % lon + 128))
        left = pltpu.roll(jnp.concatenate([before, mid], axis=1), 1, 1)[:, 128:]
        right = pltpu.roll(jnp.concatenate([mid, after], axis=1), chunk + 127, 1)[:, :chunk]
        return mid, left, right

    def sweep_block(src, dst, s, r, lift, pad):
        r = r + PAD
        here, next_row, last_row = slice(r, r + 8), slice(r + 1, r + 9), slice(r - 1, r + 7)
        for k in range(4):
            lanes = slice(k * chunk, (k + 1) * chunk)
            h, left, right = beside(lambda cols: he[s + 1, here, cols], k)
            ws = [
                h + he[s + 2, here, lanes],
                h + he[s, here, lanes],
                h + he[s + 1, next_row, lanes],
                h + he[s + 1, last_row, lanes],
                h + left,
                h + right,
            ]
            rate = 0.8 / (1.0 + (((ws[0] + ws[1]) + (ws[2] + ws[3])) + (ws[4] + ws[5])))
            for c in range(comps):
                u, left, right = beside(lambda cols: src[c, s + 1, here, cols], k)
                total = fv[c, s, r - PAD:r - PAD + 8, lanes]
                total = total + ws[0] * src[c, s + 2, here, lanes]
                total = total + ws[1] * src[c, s, here, lanes]
                total = total + ws[2] * src[c, s + 1, next_row, lanes]
                total = total + ws[3] * src[c, s + 1, last_row, lanes]
                total = total + ws[4] * left
                total = total + ws[5] * right
                dst[c, s + lift, r - PAD + pad:r - PAD + pad + 8, lanes] = 0.2 * u + rate * total

    c_force.wait()

    edge_rows = sorted({0, rows - 8})
    inner_rows = list(range(8, rows - 8, 8))

    def edges(s, carry):
        for r in edge_rows:
            sweep_block(u0, u1, s, r, 1, PAD)
        return carry

    lax.fori_loop(0, shells, edges, 0)

    @pl.when(above)
    def _():
        he_up.wait_send()
        d_up.wait_send()

    @pl.when(below)
    def _():
        he_down.wait_send()
        d_down.wait_send()

    @pl.when(south)
    def _():
        r_south.wait_send()
        e_south.wait_send()

    @pl.when(north)
    def _():
        r_north.wait_send()
        e_north.wait_send()

    g_up = remote(u1.at[:, shells, inner], u1.at[:, 0, inner], 8, "radial", up_id)
    g_down = remote(u1.at[:, 1, inner], u1.at[:, shells + 1, inner], 9, "radial", down_id)

    def stage_later(side, row):
        for c in range(comps):
            for s in range(shells):
                l_out[side, c * shells + s, :] = u1[c, s + 1, PAD + row, :]

    def unstage_later(side, row):
        for c in range(comps):
            for s in range(shells):
                u1[c, s + 1, row, :] = l_in[side, c * shells + s, :]

    s_south = remote(l_out.at[0], l_in.at[0], 10, "lateral", south_id)
    s_north = remote(l_out.at[1], l_in.at[1], 11, "lateral", north_id)
    stage_later(0, rows - 1)
    stage_later(1, 0)

    @pl.when(south)
    def _():
        s_south.start()

    @pl.when(north)
    def _():
        s_north.start()

    def insides(i, carry):
        s = i + jnp.where(above, 1, 0) * (shells - 1 - 2 * i)
        for r in inner_rows:
            sweep_block(u0, u1, s, r, 1, PAD)

        @pl.when(jnp.logical_and(above, s == shells - 1))
        def _():
            g_up.start()

        @pl.when(jnp.logical_and(below, s == 0))
        def _():
            g_down.start()

        return carry

    lax.fori_loop(0, shells, insides, 0)

    last = shells - 1
    top = place == rad - 1

    def second(s, carry):
        for r in range(0, rows, 8):
            sweep_block(u1, out, s, r, 0, 0)
        return carry

    @pl.when(above)
    def _():
        g_down.wait_recv()

    for r in inner_rows:
        sweep_block(u1, out, last, r, 0, 0)

    @pl.when(north)
    def _():
        s_south.wait_recv()
        unstage_later(0, PAD - 1)

    @pl.when(south)
    def _():
        s_north.wait_recv()
        unstage_later(1, PAD + rows)

    for r in edge_rows:
        sweep_block(u1, out, last, r, 0, 0)
    for copy in c_tables:
        copy.wait()

    quarter = lon // 4
    modes = th.shape[1] // 2
    wave = lax.broadcasted_iota(jnp.int32, (rows, modes), 1) & 3
    zero, one = jnp.zeros((rows, modes), f32), jnp.ones((rows, modes), f32)
    e1 = jnp.where(wave == 0, one, jnp.where(wave == 2, -one, zero))
    s1 = jnp.where(wave == 1, one, jnp.where(wave == 3, -one, zero))
    e2 = jnp.where((wave & 1) == 0, one, -one)
    half = width // rad
    forward = []
    for d, e in [(d, e) for d in range(lat) for e in range(rad) if d or e != rad - 1]:
        peer = lax.rem(me + d, lat)
        forward.append((d, e, pltpu.make_async_remote_copy(
            src_ref=fsend.at[peer, e], dst_ref=frecv.at[me],
            send_sem=a_send.at[d * rad + e], recv_sem=a_recv.at[d],
            device_id={"lateral": peer, "radial": e}, device_id_type=MESH)))

    @pl.when(top)
    def _():
        x = jnp.concatenate([out[0, last, :, quarter * m:quarter * (m + 1)] for m in range(4)], axis=0)
        xh, xl = split(x)
        g = dot(xh, th_v[...]) + dot(xl, th_v[...]) + dot(xh, tl_v[...])
        gc = [g[rows * m:rows * (m + 1), :modes] for m in range(4)]
        gs = [g[rows * m:rows * (m + 1), modes:] for m in range(4)]
        fc = gc[0] + e2 * gc[2] + e1 * (gc[1] + gc[3]) - s1 * (gs[1] - gs[3])
        fs = gs[0] + e2 * gs[2] + e1 * (gs[1] + gs[3]) + s1 * (gc[1] - gc[3])
        fourier = jnp.concatenate([fc, fs], axis=1)
        for p in range(lat):
            for e in range(rad):
                fsend[p, e] = fourier[:, p * width + e * half:p * width + (e + 1) * half]
        for _, _, copy in forward:
            copy.start()
        frecv[me] = fsend[me, rad - 1]

    @pl.when(below)
    def _():
        g_up.wait_recv()

    lax.fori_loop(0, last, second, 0)

    @pl.when(top)
    def _():
        for d, e, copy in forward:
            if e == rad - 1:
                copy.wait_recv()
        for _, _, copy in forward:
            copy.wait_send()

    @pl.when(jnp.logical_not(top))
    def _():
        for d, e, copy in forward:
            if e == 0:
                copy.wait_recv()

    field = frecv[...].reshape(lat * rows, half)
    fh, fl = split(field)
    coef = dot(cth_v[...], fh) + dot(cth_v[...], fl) + dot(ctl_v[...], fh)
    answer = resp_v[:, :half]
    for e in range(1, rad):
        answer = jnp.where(place == e, resp_v[:, e * half:(e + 1) * half], answer)
    sh, sl = split(answer * coef)
    load_rows = dot(ch_v[...], sh) + dot(ch_v[...], sl) + dot(cl_v[...], sh)
    gsend[...] = load_rows.reshape(lat, rows, half)
    back = []
    for d, e in offsets:
        back.append(pltpu.make_async_remote_copy(
            src_ref=gsend.at[lax.rem(me + d, lat)], dst_ref=grecv.at[me, place],
            send_sem=b_send.at[d * rad + e], recv_sem=b_recv.at[d * rad + e],
            device_id=around(d, e), device_id_type=MESH))
    for copy in back:
        copy.start()
    grecv[me, place] = gsend[me]
    coef_out[...] = coef.T
    for copy in back:
        copy.wait()
    for p in range(lat):
        for e in range(rad):
            gather[:, p * width + e * half:p * width + (e + 1) * half] = grecv[p, e]
    rc, rs = gather[:, :modes], gather[:, modes:]
    twisted = [
        (rc, rs),
        (e1 * rc + s1 * rs, e1 * rs - s1 * rc),
        (e2 * rc, e2 * rs),
        (e1 * rc - s1 * rs, e1 * rs + s1 * rc),
    ]
    a = jnp.concatenate([jnp.concatenate(pair, axis=1) for pair in twisted], axis=0)
    ah, al = split(a)
    nt = (((1,), (1,)), ((), ()))
    sea = dot(ah, th_v[...], nt) + dot(al, th_v[...], nt) + dot(ah, tl_v[...], nt)
    for m in range(4):
        cut = slice(quarter * m, quarter * (m + 1))
        sea_out[:, cut] = mask_v[:, cut].astype(f32) * sea[rows * m:rows * (m + 1)]

    @pl.when(south)
    def _():
        s_south.wait_send()

    @pl.when(north)
    def _():
        s_north.wait_send()

    @pl.when(above)
    def _():
        g_up.wait_send()

    @pl.when(below)
    def _():
        g_down.wait_send()


def writer(a, b, c, a_out, b_out, c_out, sem):
    copies = [
        pltpu.make_async_copy(source, target, sem.at[i])
        for i, (source, target) in enumerate([(a, a_out), (b, b_out), (c, c_out)])
    ]
    for copy in copies:
        copy.start()
    for copy in copies:
        copy.wait()


def shards(lat, rad, disp, force, visc, layer, response, mask):
    comps, shells, rows, lon = disp.shape
    width = response.shape[1]
    th, tl = longitude_quarter(lon, MODES)
    ch, cl = colatitude_table(lat * rows, MODES)
    tables = [th, tl, ch, cl, ch.T.copy(), cl.T.copy()]
    hbm = pl.BlockSpec(memory_space=pltpu.HBM)
    vmem = pl.BlockSpec(memory_space=pltpu.VMEM)
    field = pltpu.VMEM((comps, shells + 2, rows + 2 * PAD, lon), f32)
    staged = [pltpu.VMEM((2, n, lon), f32) for n in (comps * shells, shells, comps * shells) for _ in range(2)]
    half = width // rad
    block = pltpu.VMEM((lat, rows, half), f32)
    dma = pltpu.SemaphoreType.DMA
    spare = 4 * (disp.size + MODES * width // rad + rows * lon) + 65536
    out, coef, sea = pl.pallas_call(
        functools.partial(kernel, lat, rad, visc.shape[0]),
        out_shape=(
            pltpu.VMEM(disp.shape, f32),
            pltpu.VMEM((width // rad, MODES), f32),
            pltpu.VMEM((rows, lon), f32),
        ),
        in_specs=[hbm, hbm, pl.BlockSpec(memory_space=pltpu.SMEM)] + [hbm] * 9,
        out_specs=(vmem, vmem, vmem),
        scratch_shapes=[
            field, field,
            pltpu.VMEM((comps, shells, rows, lon), f32),
            pltpu.VMEM((shells, rows, lon), jnp.int32),
            pltpu.VMEM((shells + 2, rows + 2 * PAD, lon), f32),
            *staged,
            pltpu.VMEM((lat, rad, rows, half), f32), block, block, pltpu.VMEM((lat, rad, rows, half), f32),
            pltpu.VMEM((rows, 2 * MODES), f32),
            pltpu.VMEM(response.shape, f32), pltpu.VMEM(mask.shape, jnp.int32),
        ] + [pltpu.VMEM(t.shape, bf16) for t in tables] + [
            dma((11,)), dma((12,)), dma((12,)), dma((lat * rad,)), dma((lat,)),
            dma((lat * rad,)), dma((lat * rad,)),
        ],
        compiler_params=pltpu.CompilerParams(
            collective_id=0, has_side_effects=True, vmem_limit_bytes=VMEM - spare),
    )(disp, force, visc, layer, response, mask, *[jnp.asarray(t) for t in tables])
    out, coef, sea = pl.pallas_call(
        writer,
        out_shape=tuple(jax.ShapeDtypeStruct(a.shape, f32) for a in (out, coef, sea)),
        in_specs=[vmem] * 3,
        out_specs=(hbm, hbm, hbm),
        scratch_shapes=[dma((3,))],
        compiler_params=pltpu.CompilerParams(vmem_limit_bytes=1 << 20),
    )(out, coef, sea)
    return out, coef.T, sea


def solution(mesh):
    in_specs = (
        P("member", "radial", "lateral", None),
        P("member", "radial", "lateral", None),
        P("member"),
        P("radial", "lateral", None),
        P(None, "lateral"),
        P("lateral", None),
    )
    out_specs = (
        P("member", "radial", "lateral", None),
        P("member", ("lateral", "radial")),
        P("lateral", "member"),
    )
    body = functools.partial(shards, mesh.shape["lateral"], mesh.shape["radial"])
    return jax.shard_map(body, mesh=mesh, in_specs=in_specs, out_specs=out_specs, check_vma=False)
```

```python
import functools
import math

import jax
import jax.numpy as jnp
import ml_dtypes
import numpy as np
from jax import lax
from jax.experimental import pallas as pl
from jax.experimental.pallas import tpu as pltpu
from jax.sharding import PartitionSpec as P

MODES = 512
PAD = 8
VMEM = 67043328
MESH = pl.DeviceIdType.MESH
f32, bf16 = jnp.float32, jnp.bfloat16


def halves(table):
    table = table.astype(np.float32)
    high = table.astype(ml_dtypes.bfloat16)
    low = (table - high.astype(np.float32)).astype(ml_dtypes.bfloat16)
    return high, low


def longitude_quarter(count, modes):
    points = np.arange(count // 4)[:, None]
    phase = points * np.arange(modes)[None, :] % count
    angle = 2.0 * math.pi / count * phase
    table = np.concatenate([np.cos(angle), np.sin(angle)], axis=1)
    return halves(table * math.sqrt(2.0 / count))


def colatitude_table(count, modes):
    points = np.arange(count)[:, None]
    phase = np.arange(modes)[None, :] * (2 * points + 1) % (4 * count)
    table = np.cos(math.pi / (2 * count) * phase) * math.sqrt(2.0 / count)
    return halves(table)


def split(x):
    high = x.astype(bf16)
    return high, (x - high.astype(f32)).astype(bf16)


def dot(a, b, dims=(((1,), (0,)), ((), ()))):
    return lax.dot_general(a, b, dims, preferred_element_type=f32)


def choose(index, values):
    bit = 0
    while len(values) > 1:
        odd = (index & (1 << bit)) != 0
        values = [
            jnp.where(odd, values[min(i + 1, len(values) - 1)], values[i])
            for i in range(0, len(values), 2)
        ]
        bit += 1
    return values[0]


def kernel(lat, rad, layers, disp, force, visc, layer, response, mask, th, tl, ch, cl, cth, ctl,
           out, coef_out, sea_out,
           u0, u1, fv, li, he, r_out, r_in, e_out, e_in, l_out, l_in, fsend, frecv, gsend, grecv, gather,
           resp_v, mask_v, th_v, tl_v, ch_v, cl_v, cth_v, ctl_v,
           load_sem, send_sem, recv_sem, a_send, a_recv, b_send, b_recv):
    comps, shells, rows, lon = disp.shape
    width = response.shape[1]
    me = lax.axis_index("lateral")
    place = lax.axis_index("radial")
    inner = pl.ds(PAD, rows)

    def load(source, target, index):
        copy = pltpu.make_async_copy(source, target, load_sem.at[index])
        copy.start()
        return copy

    c_layer = load(layer, li, 0)
    c_disp = load(disp, u0.at[:, pl.ds(1, shells), inner], 1)
    c_force = load(force, fv, 2)
    pairs = [(response, resp_v), (mask, mask_v), (th, th_v), (tl, tl_v), (ch, ch_v), (cl, cl_v),
             (cth, cth_v), (ctl, ctl_v)]
    def around(d, e):
        return {"lateral": lax.rem(me + d, lat), "radial": lax.rem(place + e, rad)}

    barrier = pltpu.get_barrier_semaphore()
    offsets = [(d, e) for d in range(lat) for e in range(rad) if d or e]
    for d, e in offsets:
        pl.semaphore_signal(barrier, inc=1, device_id=around(d, e), device_id_type=MESH)

    def remote(source, target, sem, axis, where):
        return pltpu.make_async_remote_copy(
            src_ref=source, dst_ref=target, send_sem=send_sem.at[sem], recv_sem=recv_sem.at[sem],
            device_id={axis: where}, device_id_type=MESH)

    above, below = place < rad - 1, place > 0
    south, north = me < lat - 1, me > 0
    up_id, down_id = lax.rem(place + 1, rad), lax.rem(place + rad - 1, rad)
    south_id, north_id = lax.rem(me + 1, lat), lax.rem(me + lat - 1, lat)

    he_up = remote(he.at[shells, inner], he.at[0, inner], 0, "radial", up_id)
    he_down = remote(he.at[1, inner], he.at[shells + 1, inner], 1, "radial", down_id)
    d_up = remote(disp.at[:, shells - 1], u0.at[:, 0, inner], 2, "radial", up_id)
    d_down = remote(disp.at[:, 0], u0.at[:, shells + 1, inner], 3, "radial", down_id)

    values = [visc[i] * 0.5 for i in range(layers)]

    def lookup(s):
        for r in range(0, rows, 8):
            he[s, PAD + r:PAD + r + 8, :] = choose(li[s - 1, r:r + 8, :], values)

    def lookup_step(i, carry):
        lookup(i + 1)
        return carry

    def stage(field, side, row):
        for c in range(comps):
            for s in range(shells):
                r_out[side, c * shells + s, :] = field[c, s + 1, PAD + row, :]

    def unstage(field, side, row):
        for c in range(comps):
            for s in range(shells):
                field[c, s + 1, row, :] = r_in[side, c * shells + s, :]

    def unstage_zero(field, row):
        for c in range(comps):
            for s in range(shells):
                field[c, s + 1, row, :] = jnp.zeros((lon,), f32)

    c_disp.wait()
    c_tables = [load(a, b, 3 + i) for i, (a, b) in enumerate(pairs)]
    stage(u0, 0, rows - 1)
    stage(u0, 1, 0)
    r_south = remote(r_out.at[0], r_in.at[0], 4, "lateral", south_id)
    r_north = remote(r_out.at[1], r_in.at[1], 5, "lateral", north_id)

    c_layer.wait()
    lax.fori_loop(0, shells, lookup_step, 0)
    for s in range(shells):
        e_out[0, s, :] = he[s + 1, PAD + rows - 1, :]
        e_out[1, s, :] = he[s + 1, PAD, :]
    e_south = remote(e_out.at[0], e_in.at[0], 6, "lateral", south_id)
    e_north = remote(e_out.at[1], e_in.at[1], 7, "lateral", north_id)

    pl.semaphore_wait(barrier, lat * rad - 1)

    @pl.when(south)
    def _():
        r_south.start()
        e_south.start()

    @pl.when(north)
    def _():
        r_north.start()
        e_north.start()

    @pl.when(above)
    def _():
        he_up.start()
        d_up.start()

    @pl.when(below)
    def _():
        he_down.start()
        d_down.start()

    @pl.when(below)
    def _():
        he_up.wait_recv()
        d_up.wait_recv()

    @pl.when(jnp.logical_not(below))
    def _():
        he[0, PAD:PAD + rows, :] = jnp.zeros((rows, lon), f32)
        for c in range(comps):
            u0[c, 0, PAD:PAD + rows, :] = jnp.zeros((rows, lon), f32)
            u1[c, 0, PAD:PAD + rows, :] = jnp.zeros((rows, lon), f32)

    @pl.when(above)
    def _():
        he_down.wait_recv()
        d_down.wait_recv()

    @pl.when(jnp.logical_not(above))
    def _():
        he[shells + 1, PAD:PAD + rows, :] = jnp.zeros((rows, lon), f32)
        for c in range(comps):
            u0[c, shells + 1, PAD:PAD + rows, :] = jnp.zeros((rows, lon), f32)
            u1[c, shells + 1, PAD:PAD + rows, :] = jnp.zeros((rows, lon), f32)

    @pl.when(north)
    def _():
        r_south.wait_recv()
        e_south.wait_recv()
        unstage(u0, 0, PAD - 1)
        for s in range(shells):
            he[s + 1, PAD - 1, :] = e_in[0, s, :]

    @pl.when(jnp.logical_not(north))
    def _():
        unstage_zero(u0, PAD - 1)
        unstage_zero(u1, PAD - 1)
        for s in range(shells):
            he[s + 1, PAD - 1, :] = jnp.zeros((lon,), f32)

    @pl.when(south)
    def _():
        r_north.wait_recv()
        e_north.wait_recv()
        unstage(u0, 1, PAD + rows)
        for s in range(shells):
            he[s + 1, PAD + rows, :] = e_in[1, s, :]

    @pl.when(jnp.logical_not(south))
    def _():
        unstage_zero(u0, PAD + rows)
        unstage_zero(u1, PAD + rows)
        for s in range(shells):
            he[s + 1, PAD + rows, :] = jnp.zeros((lon,), f32)

    chunk = lon // 4

    def beside(load, k):
        first, end = k * chunk, (k + 1) * chunk
        mid = load(slice(first, end))
        before = load(slice((first - 128) % lon, (first - 128) % lon + 128))
        after = load(slice(end % lon, end % lon + 128))
        left = pltpu.roll(jnp.concatenate([before, mid], axis=1), 1, 1)[:, 128:]
        right = pltpu.roll(jnp.concatenate([mid, after], axis=1), chunk + 127, 1)[:, :chunk]
        return mid, left, right

    def sweep_block(src, dst, s, r, lift, pad):
        r = r + PAD
        here, later, earlier = slice(r, r + 8), slice(r + 8, r + 16), slice(r - 8, r)
        row = lax.broadcasted_iota(jnp.int32, (8, chunk), 0)
        first_row, final_row = row == 0, row == 7

        def rows_beside(load, mid):
            following = pltpu.roll(jnp.where(first_row, load(later), mid), 7, 0)
            leading = pltpu.roll(jnp.where(final_row, load(earlier), mid), 1, 0)
            return following, leading

        for k in range(lon // chunk):
            lanes = slice(k * chunk, (k + 1) * chunk)
            h, left, right = beside(lambda cols: he[s + 1, here, cols], k)
            following, leading = rows_beside(lambda at: he[s + 1, at, lanes], h)
            ws = [
                h + he[s + 2, here, lanes],
                h + he[s, here, lanes],
                h + following,
                h + leading,
                h + left,
                h + right,
            ]
            rate = 0.8 / (1.0 + (((ws[0] + ws[1]) + (ws[2] + ws[3])) + (ws[4] + ws[5])))
            for c in range(comps):
                u, left, right = beside(lambda cols: src[c, s + 1, here, cols], k)
                following, leading = rows_beside(lambda at: src[c, s + 1, at, lanes], u)
                total = fv[c, s, r - PAD:r - PAD + 8, lanes]
                total = total + ws[0] * src[c, s + 2, here, lanes]
                total = total + ws[1] * src[c, s, here, lanes]
                total = total + ws[2] * following
                total = total + ws[3] * leading
                total = total + ws[4] * left
                total = total + ws[5] * right
                dst[c, s + lift, r - PAD + pad:r - PAD + pad + 8, lanes] = 0.2 * u + rate * total

    c_force.wait()

    edge_rows = sorted({0, rows - 8})
    inner_rows = list(range(8, rows - 8, 8))

    def edges(s, carry):
        for r in edge_rows:
            sweep_block(u0, u1, s, r, 1, PAD)
        return carry

    lax.fori_loop(0, shells, edges, 0)

    @pl.when(above)
    def _():
        he_up.wait_send()
        d_up.wait_send()

    @pl.when(below)
    def _():
        he_down.wait_send()
        d_down.wait_send()

    @pl.when(south)
    def _():
        r_south.wait_send()
        e_south.wait_send()

    @pl.when(north)
    def _():
        r_north.wait_send()
        e_north.wait_send()

    g_up = remote(u1.at[:, shells, inner], u1.at[:, 0, inner], 8, "radial", up_id)
    g_down = remote(u1.at[:, 1, inner], u1.at[:, shells + 1, inner], 9, "radial", down_id)

    def stage_later(side, row):
        for c in range(comps):
            for s in range(shells):
                l_out[side, c * shells + s, :] = u1[c, s + 1, PAD + row, :]

    def unstage_later(side, row):
        for c in range(comps):
            for s in range(shells):
                u1[c, s + 1, row, :] = l_in[side, c * shells + s, :]

    s_south = remote(l_out.at[0], l_in.at[0], 10, "lateral", south_id)
    s_north = remote(l_out.at[1], l_in.at[1], 11, "lateral", north_id)
    stage_later(0, rows - 1)
    stage_later(1, 0)

    @pl.when(south)
    def _():
        s_south.start()

    @pl.when(north)
    def _():
        s_north.start()

    def insides(i, carry):
        s = i + jnp.where(above, 1, 0) * (shells - 1 - 2 * i)
        for r in inner_rows:
            sweep_block(u0, u1, s, r, 1, PAD)

        @pl.when(jnp.logical_and(above, s == shells - 1))
        def _():
            g_up.start()

        @pl.when(jnp.logical_and(below, s == 0))
        def _():
            g_down.start()

        return carry

    lax.fori_loop(0, shells, insides, 0)

    last = shells - 1
    top = place == rad - 1

    def second(s, carry):
        for r in range(0, rows, 8):
            sweep_block(u1, out, s, r, 0, 0)
        return carry

    @pl.when(above)
    def _():
        g_down.wait_recv()

    for r in inner_rows:
        sweep_block(u1, out, last, r, 0, 0)

    @pl.when(north)
    def _():
        s_south.wait_recv()
        unstage_later(0, PAD - 1)

    @pl.when(south)
    def _():
        s_north.wait_recv()
        unstage_later(1, PAD + rows)

    for r in edge_rows:
        sweep_block(u1, out, last, r, 0, 0)
    for copy in c_tables:
        copy.wait()

    quarter = lon // 4
    modes = th.shape[1] // 2
    wave = lax.broadcasted_iota(jnp.int32, (rows, modes), 1) & 3
    zero, one = jnp.zeros((rows, modes), f32), jnp.ones((rows, modes), f32)
    e1 = jnp.where(wave == 0, one, jnp.where(wave == 2, -one, zero))
    s1 = jnp.where(wave == 1, one, jnp.where(wave == 3, -one, zero))
    e2 = jnp.where((wave & 1) == 0, one, -one)
    half = width // rad
    forward = []
    for d, e in [(d, e) for d in range(lat) for e in range(rad) if d or e != rad - 1]:
        peer = lax.rem(me + d, lat)
        forward.append((d, e, pltpu.make_async_remote_copy(
            src_ref=fsend.at[peer, e], dst_ref=frecv.at[me],
            send_sem=a_send.at[d * rad + e], recv_sem=a_recv.at[d],
            device_id={"lateral": peer, "radial": e}, device_id_type=MESH)))

    @pl.when(top)
    def _():
        x = jnp.concatenate([out[0, last, :, quarter * m:quarter * (m + 1)] for m in range(4)], axis=0)
        xh, xl = split(x)
        g = dot(xh, th_v[...]) + dot(xl, th_v[...]) + dot(xh, tl_v[...])
        gc = [g[rows * m:rows * (m + 1), :modes] for m in range(4)]
        gs = [g[rows * m:rows * (m + 1), modes:] for m in range(4)]
        fc = gc[0] + e2 * gc[2] + e1 * (gc[1] + gc[3]) - s1 * (gs[1] - gs[3])
        fs = gs[0] + e2 * gs[2] + e1 * (gs[1] + gs[3]) + s1 * (gc[1] - gc[3])
        fourier = jnp.concatenate([fc, fs], axis=1)
        for p in range(lat):
            for e in range(rad):
                fsend[p, e] = fourier[:, p * width + e * half:p * width + (e + 1) * half]
        for _, _, copy in forward:
            copy.start()
        frecv[me] = fsend[me, rad - 1]

    @pl.when(below)
    def _():
        g_up.wait_recv()

    lax.fori_loop(0, last, second, 0)

    @pl.when(top)
    def _():
        for d, e, copy in forward:
            if e == rad - 1:
                copy.wait_recv()
        for _, _, copy in forward:
            copy.wait_send()

    @pl.when(jnp.logical_not(top))
    def _():
        for d, e, copy in forward:
            if e == 0:
                copy.wait_recv()

    field = frecv[...].reshape(lat * rows, half)
    fh, fl = split(field)
    coef = dot(cth_v[...], fh) + dot(cth_v[...], fl) + dot(ctl_v[...], fh)
    answer = resp_v[:, :half]
    for e in range(1, rad):
        answer = jnp.where(place == e, resp_v[:, e * half:(e + 1) * half], answer)
    sh, sl = split(answer * coef)
    load_rows = dot(ch_v[...], sh) + dot(ch_v[...], sl) + dot(cl_v[...], sh)
    gsend[...] = load_rows.reshape(lat, rows, half)
    back = []
    for d, e in offsets:
        back.append(pltpu.make_async_remote_copy(
            src_ref=gsend.at[lax.rem(me + d, lat)], dst_ref=grecv.at[me, place],
            send_sem=b_send.at[d * rad + e], recv_sem=b_recv.at[d * rad + e],
            device_id=around(d, e), device_id_type=MESH))
    for copy in back:
        copy.start()
    grecv[me, place] = gsend[me]
    coef_out[...] = coef.T
    for copy in back:
        copy.wait()
    for p in range(lat):
        for e in range(rad):
            gather[:, p * width + e * half:p * width + (e + 1) * half] = grecv[p, e]
    rc, rs = gather[:, :modes], gather[:, modes:]
    twisted = [
        (rc, rs),
        (e1 * rc + s1 * rs, e1 * rs - s1 * rc),
        (e2 * rc, e2 * rs),
        (e1 * rc - s1 * rs, e1 * rs + s1 * rc),
    ]
    a = jnp.concatenate([jnp.concatenate(pair, axis=1) for pair in twisted], axis=0)
    ah, al = split(a)
    nt = (((1,), (1,)), ((), ()))
    sea = dot(ah, th_v[...], nt) + dot(al, th_v[...], nt) + dot(ah, tl_v[...], nt)
    for m in range(4):
        cut = slice(quarter * m, quarter * (m + 1))
        sea_out[:, cut] = mask_v[:, cut].astype(f32) * sea[rows * m:rows * (m + 1)]

    @pl.when(south)
    def _():
        s_south.wait_send()

    @pl.when(north)
    def _():
        s_north.wait_send()

    @pl.when(above)
    def _():
        g_up.wait_send()

    @pl.when(below)
    def _():
        g_down.wait_send()


def writer(a, b, c, a_out, b_out, c_out, sem):
    copies = [
        pltpu.make_async_copy(source, target, sem.at[i])
        for i, (source, target) in enumerate([(a, a_out), (b, b_out), (c, c_out)])
    ]
    for copy in copies:
        copy.start()
    for copy in copies:
        copy.wait()


def shards(lat, rad, disp, force, visc, layer, response, mask):
    comps, shells, rows, lon = disp.shape
    width = response.shape[1]
    th, tl = longitude_quarter(lon, MODES)
    ch, cl = colatitude_table(lat * rows, MODES)
    tables = [th, tl, ch, cl, ch.T.copy(), cl.T.copy()]
    hbm = pl.BlockSpec(memory_space=pltpu.HBM)
    vmem = pl.BlockSpec(memory_space=pltpu.VMEM)
    field = pltpu.VMEM((comps, shells + 2, rows + 2 * PAD, lon), f32)
    staged = [pltpu.VMEM((2, n, lon), f32) for n in (comps * shells, shells, comps * shells) for _ in range(2)]
    half = width // rad
    block = pltpu.VMEM((lat, rows, half), f32)
    dma = pltpu.SemaphoreType.DMA
    spare = 4 * (disp.size + MODES * width // rad + rows * lon) + 65536
    out, coef, sea = pl.pallas_call(
        functools.partial(kernel, lat, rad, visc.shape[0]),
        out_shape=(
            pltpu.VMEM(disp.shape, f32),
            pltpu.VMEM((width // rad, MODES), f32),
            pltpu.VMEM((rows, lon), f32),
        ),
        in_specs=[hbm, hbm, pl.BlockSpec(memory_space=pltpu.SMEM)] + [hbm] * 9,
        out_specs=(vmem, vmem, vmem),
        scratch_shapes=[
            field, field,
            pltpu.VMEM((comps, shells, rows, lon), f32),
            pltpu.VMEM((shells, rows, lon), jnp.int32),
            pltpu.VMEM((shells + 2, rows + 2 * PAD, lon), f32),
            *staged,
            pltpu.VMEM((lat, rad, rows, half), f32), block, block, pltpu.VMEM((lat, rad, rows, half), f32),
            pltpu.VMEM((rows, 2 * MODES), f32),
            pltpu.VMEM(response.shape, f32), pltpu.VMEM(mask.shape, jnp.int32),
        ] + [pltpu.VMEM(t.shape, bf16) for t in tables] + [
            dma((11,)), dma((12,)), dma((12,)), dma((lat * rad,)), dma((lat,)),
            dma((lat * rad,)), dma((lat * rad,)),
        ],
        compiler_params=pltpu.CompilerParams(
            collective_id=0, has_side_effects=True, vmem_limit_bytes=VMEM - spare),
    )(disp, force, visc, layer, response, mask, *[jnp.asarray(t) for t in tables])
    out, coef, sea = pl.pallas_call(
        writer,
        out_shape=tuple(jax.ShapeDtypeStruct(a.shape, f32) for a in (out, coef, sea)),
        in_specs=[vmem] * 3,
        out_specs=(hbm, hbm, hbm),
        scratch_shapes=[dma((3,))],
        compiler_params=pltpu.CompilerParams(vmem_limit_bytes=1 << 20),
    )(out, coef, sea)
    return out, coef.T, sea


def solution(mesh):
    in_specs = (
        P("member", "radial", "lateral", None),
        P("member", "radial", "lateral", None),
        P("member"),
        P("radial", "lateral", None),
        P(None, "lateral"),
        P("lateral", None),
    )
    out_specs = (
        P("member", "radial", "lateral", None),
        P("member", ("lateral", "radial")),
        P("lateral", "member"),
    )
    body = functools.partial(shards, mesh.shape["lateral"], mesh.shape["radial"])
    return jax.shard_map(body, mesh=mesh, in_specs=in_specs, out_specs=out_specs, check_vma=False)
```
